128 devices in a mesh: seq: 32 (over z, y, core), head: 4 (over x).
Axes of the slice: x: 4, y: 4, z: 4, core: 2. Of those that a mesh axis runs over, the one named last changes fastest.
Arguments:
- tokens: bfloat16 [32768, 2048], P('seq'), may hold values from -6 to 6
- w_query: bfloat16 [2048, 2048], P(None, 'head'), may hold values from -0.125 to 0.125
- w_key: bfloat16 [2048, 2048], P(None, 'head'), may hold values from -0.125 to 0.125
- w_value: bfloat16 [2048, 2048], P(None, 'head'), may hold values from -0.125 to 0.125
- omega: float32 [128, 256], replicated, may hold values from -5 to 5
- w_out: bfloat16 [2048, 2048], P('head'), may hold values from -0.125 to 0.125
Outputs:
- mixed: bfloat16 [32768, 2048], P(('seq', 'head'))
The draws below stay inside these ranges and needn't reach their ends.
All inputs are finite; a program needn't handle non-finite values.
Results may differ from the reference program's by a relative error of at most 0.0063.
Values may be sent and summed in bfloat16 or wider, within the bound.
A program may use at most 128 MiB of HBM per device.

```python
import math
import jax
import jax.numpy as jnp
from jax import lax

D = 2048
HEADS = 16
DH = 128
M = 256
BLOCK = 512
TOKENS = 32768


def block_levels(stream_key, dims, cuts, least, top_value):
    gain = 1.0
    for axis_at, blocks in cuts:
        heights = jax.random.uniform(jax.random.fold_in(jax.random.fold_in(stream_key, 6), axis_at), (blocks,), jnp.float32, least / len(cuts), top_value / len(cuts))
        gain = gain * jnp.repeat(jnp.exp(heights), dims[axis_at] // blocks).reshape((-1,) + (1,) * (len(dims) - 1 - axis_at))
    return gain


def gaussian(rng, extent, deviation, bound, cuts=(), kind=jnp.bfloat16):
    level = block_levels(rng, extent, cuts, -0.22, 0.18) if cuts else 1.0
    entries = jax.random.normal(rng, extent, jnp.float32) * deviation * level
    return jnp.minimum(jnp.maximum(entries, -bound), bound).astype(kind)


def setup_inputs(seed: int = 0) -> dict:
    splits = jax.random.split(jax.random.key(seed), 7)
    return {
        "tokens": gaussian(splits[0], (TOKENS, D), 1.0, 6.0, ((0, 32),)),
        "w_query": gaussian(splits[1], (D, HEADS * DH), D ** -0.5, 0.125, ((1, 4),)),
        "w_key": gaussian(splits[2], (D, HEADS * DH), D ** -0.5, 0.125, ((1, 4),)),
        "w_value": gaussian(splits[3], (D, HEADS * DH), D ** -0.5, 0.125, ((1, 4),)),
        "omega": gaussian(splits[4], (DH, M), 1.0, 5.0, (), jnp.float32),
        "w_out": gaussian(splits[5], (HEADS * DH, D), (HEADS * DH) ** -0.5, 0.125, ((0, 4),)),
    }


highest_precision = lax.Precision.HIGHEST
stabilizer = 0.001

def feature_map(values, omega):
    scaled = values * DH ** (-0.25)
    projected = jnp.einsum('thd,dm->thm', scaled, omega, precision=highest_precision)
    half_square = 0.5 * lax.optimization_barrier(jnp.sum(scaled * scaled, axis=-1, keepdims=True))
    return ((jnp.exp(projected - half_square) + stabilizer) / math.sqrt(M)).astype(jnp.bfloat16)

def reference(tokens, w_query, w_key, w_value, omega, w_out):
    length = tokens.shape[0]
    query = jnp.dot(tokens, w_query, preferred_element_type=jnp.float32).reshape(length, HEADS, DH)
    key = jnp.dot(tokens, w_key, preferred_element_type=jnp.float32).reshape(length, HEADS, DH)
    value = jnp.dot(tokens, w_value, preferred_element_type=jnp.float32).astype(jnp.bfloat16).reshape(length, HEADS, DH)
    query_feat = feature_map(query, omega)
    key_feat = feature_map(key, omega)
    block_count = length // BLOCK
    query_blocks = query_feat.reshape(block_count, BLOCK, HEADS, M)
    key_blocks = key_feat.reshape(block_count, BLOCK, HEADS, M)
    value_blocks = value.reshape(block_count, BLOCK, HEADS, DH)
    causal = jnp.arange(BLOCK)[:, None] >= jnp.arange(BLOCK)[None, :]

    def advance(carry, blocks):
        state_matrix, norm = carry
        query_features = blocks[0].astype(jnp.float32)
        key_features = blocks[1].astype(jnp.float32)
        value_features = blocks[2].astype(jnp.float32)
        scores = jnp.einsum('thm,shm->hts', query_features, key_features, precision=highest_precision)
        scores = jnp.where(causal[None], scores, jnp.float32(0.0))
        denom = lax.optimization_barrier(jnp.sum(scores, axis=-1)).T + jnp.einsum('thm,hm->th', query_features, norm, precision=highest_precision)
        weights = lax.optimization_barrier(scores.astype(jnp.bfloat16)).astype(jnp.float32)
        numerator = jnp.einsum('hts,shd->thd', weights, value_features, precision=highest_precision)
        numerator = numerator + jnp.einsum('crx,rxs->crs', query_features, state_matrix, precision=highest_precision)
        attended = (numerator / denom[..., None]).astype(jnp.bfloat16)
        state_matrix = state_matrix + jnp.einsum('xtv,xte->tve', key_features, value_features, precision=highest_precision)
        norm = norm + lax.optimization_barrier(jnp.sum(key_features, axis=0))
        return ((state_matrix, norm), attended)
    start_state = (jnp.zeros((HEADS, M, DH), jnp.float32), jnp.zeros((HEADS, M), jnp.float32))
    ignored, attended = lax.scan(advance, start_state, (query_blocks, key_blocks, value_blocks))
    attention = attended.reshape(length, HEADS * DH)
    return jnp.dot(attention, w_out, preferred_element_type=jnp.float32).astype(jnp.bfloat16)
```

```python
import functools

import jax
import jax.numpy as jnp
from jax import lax
from jax.experimental import pallas as pl
from jax.experimental.pallas import tpu as pltpu
from jax.sharding import PartitionSpec as P

MESH = pl.DeviceIdType.MESH
BF, F32 = jnp.bfloat16, jnp.float32
LOG2E = 1.4426950408889634
CHUNK = 256
NORM = 16
DIRECT = 64

NT = (((1,), (1,)), ((), ()))


def dot(a, b):
    return jnp.dot(a, b, preferred_element_type=F32)


def dot_nt(a, b):
    return lax.dot_general(a, b, NT, preferred_element_type=F32)


def widen(state):
    norm = state[128:]
    return jnp.concatenate([state[:128]] + [norm] * (128 // NORM), axis=0)


def kernel(
    tok, wq, wk, wv, om, wo, out,
    tokv, wqv, wkv, wvv, wof, kf, qf, vv, omw, run, sloc, acc, res,
    sx, r0, ma, ra, ma2, ra2, mb, rb, mb2, rb2, pa, ua, pb, ps, pf, atts, attb,
    lsem, s0, q0, s1a, q1a, s1b, q1b, s2a, q2a, s2b, q2b, s3, q3, sA, qA,
    wsd, wqd, wsx, wqx, wsy, wqy, wsp, wqp,
):
    seq, x = lax.axis_index("seq"), lax.axis_index("head")
    z, y, c = lax.div(seq, 8), lax.rem(lax.div(seq, 2), 4), lax.rem(seq, 2)

    def ahead(v, o):
        return lax.rem(v + o, 4)

    def dev(z_, y_, c_, x_):
        return {"seq": z_ * 8 + y_ * 2 + c_, "head": x_}

    partner = dev(z, y, 1 - c, x)
    ydev = [dev(z, ahead(y, o), c, x) for o in (1, 2, 3)]
    zdev = [dev(ahead(z, o), y, c, x) for o in (1, 2, 3)]
    xdev = [dev(z, y, c, ahead(x, o)) for o in (1, 2, 3)]

    def remote(src, dst, ss, rs, to):
        return pltpu.make_async_remote_copy(
            src_ref=src, dst_ref=dst, send_sem=ss, recv_sem=rs, device_id=to, device_id_type=MESH
        )

    loads = [pltpu.make_async_copy(wk, wkv, lsem.at[0])]
    for j in range(4):
        loads.append(
            pltpu.make_async_copy(
                tok.at[pl.ds(j * CHUNK, CHUNK)], tokv.at[pl.ds(j * CHUNK, CHUNK)], lsem.at[1 + j]
            )
        )
        if j == 0:
            loads.append(pltpu.make_async_copy(wv, wvv, lsem.at[5]))
    loads.append(pltpu.make_async_copy(wq, wqv, lsem.at[6]))
    loads.append(pltpu.make_async_copy(wo, wof.at[x], lsem.at[7]))
    for copy in loads:
        copy.start()

    barrier = pltpu.get_barrier_semaphore()
    for to in [partner] + ydev + zdev + xdev:
        pl.semaphore_signal(barrier, inc=1, device_id=to, device_id_type=MESH)

    scale = 128.0**-0.25
    omega = om[...] * (scale * LOG2E)
    om_hi = omega.astype(BF)
    om_lo = (omega - om_hi.astype(F32)).astype(BF)
    omw[pl.ds(0, 128)] = om_hi
    omw[pl.ds(128, 128)] = om_hi
    omw[pl.ds(256, 128)] = om_lo
    omw[pl.ds(384, 128)] = jnp.full((128, 256), -1.0, BF)
    run[...] = jnp.zeros_like(run)

    low = lax.broadcasted_iota(jnp.int32, (CHUNK, 128), 1) < 64

    def features(p):
        hi = p.astype(BF)
        lo = (p - hi.astype(F32)).astype(BF)
        square = p * p * (0.5 * scale * scale * LOG2E)
        pair = square + pltpu.roll(square, 64, 1) + 4.0 / 64
        pair_hi = pair.astype(BF).astype(F32)
        sums = jnp.where(low, pair_hi, pair - pair_hi).astype(BF)
        power = dot(jnp.concatenate([hi, lo, hi, sums], axis=1), omw[...])
        return (jnp.exp2(power) + 0.001 / 16).astype(BF)

    pl.semaphore_wait(barrier, 10)

    half = c * 256
    share = (256 - DIRECT) // 4
    mine = lax.select(c == 0, y, z)
    at_direct = pl.multiple_of(half, 64)
    at_piece = pl.multiple_of(half + DIRECT + mine * share, 16)
    w_direct = [
        remote(wo.at[pl.ds(at_direct, DIRECT)], wof.at[x, pl.ds(at_direct, DIRECT)],
               wsd.at[i], wqd.at[i], xdev[i])
        for i in range(3)
    ]
    w_piece = [
        remote(wo.at[pl.ds(at_piece, share)], wof.at[x, pl.ds(at_piece, share)],
               wsx.at[i], wqx.at[i], xdev[i])
        for i in range(3)
    ]
    for copy in w_piece + w_direct:
        copy.start()

    loads[0].wait()
    loads[2].wait()

    def key_value(j):
        rows = pl.ds(pl.multiple_of(j * CHUNK, CHUNK), CHUNK)
        t = tokv[rows]
        k = dot(t, wkv[...])
        v = dot(t, wvv[...])
        vv[rows] = v.astype(BF)
        for h in range(4):
            feat = features(k[:, h * 128 : (h + 1) * 128])
            kf[rows, h * 256 : (h + 1) * 256] = feat
            turned = jnp.concatenate(
                [v[:, h * 128 : (h + 1) * 128].T.astype(BF), jnp.ones((NORM, CHUNK), BF)], axis=0
            )
            so_far = run[h]
            sloc[j, h] = so_far.astype(BF)
            run[h] = so_far + dot(turned, feat)

    for j in range(4):
        loads[1 if j == 0 else 2 + j].wait()
        key_value(j)

    first, other = 2 * c, 2 - 2 * c
    sx[...] = run[pl.ds(other, 2)].astype(BF)
    round0 = remote(sx, r0, s0, q0, partner)
    round0.start()

    causal = lax.broadcasted_iota(jnp.int32, (CHUNK, CHUNK), 0) >= lax.broadcasted_iota(
        jnp.int32, (CHUNK, CHUNK), 1
    )
    ones = jnp.ones((CHUNK, 128), BF)

    def query(j):
        rows = pl.ds(j * CHUNK, CHUNK)
        q = dot(tokv[rows], wqv[...])
        for h in range(4):
            qf[rows, h * 256 : (h + 1) * 256] = features(q[:, h * 128 : (h + 1) * 128])

    def inside(j):
        rows = pl.ds(j * CHUNK, CHUNK)
        for h in range(4):
            feat = qf[rows, h * 256 : (h + 1) * 256]
            scores = dot_nt(feat, kf[rows, h * 256 : (h + 1) * 256])
            weights = jnp.where(causal, scores, 0.0).astype(BF)
            value = jnp.concatenate([vv[rows, h * 128 : (h + 1) * 128], ones], axis=1)
            total = dot(weights, value)
            if j > 0:
                total = total + dot_nt(feat, widen(sloc[j, h]))
            acc[h, rows] = total

    loads[6].wait()
    query(0)

    round0.wait()
    chip = run[pl.ds(first, 2)] + r0[...].astype(F32)
    ua[...] = chip[:, :, :128]
    pb[...] = jnp.zeros_like(pb)
    ma[...] = chip[:, :, :128].astype(BF)
    mb[...] = chip[:, :, 128:].astype(BF)
    round1a = [remote(ma, ra.at[i], s1a.at[i], q1a.at[i], ydev[i]) for i in range(3)]
    round1b = [remote(mb, rb.at[i], s1b.at[i], q1b.at[i], zdev[i]) for i in range(3)]
    for i in range(3):
        round1a[i].start()
        pl.when(z + i + 1 < 4)(round1b[i].start)

    query(1)
    query(2)
    inside(0)

    pa[...] = jnp.zeros_like(pa)
    for i in range(3):
        round1a[i].wait()
        got = ra[i].astype(F32)
        ua[...] += got
        pa[...] += jnp.where(y >= i + 1, got, 0.0)
        pl.when(z + i + 1 < 4)(round1b[i].wait_send)

        @pl.when(z >= i + 1)
        def _():
            round1b[i].wait_recv()
            pb[...] += rb[i].astype(F32)

    ma2[...] = ua[...].astype(BF)
    mb2[0] = pb[...].astype(BF)
    mb2[1] = (pb[...] + mb[...].astype(F32)).astype(BF)
    round2a = [remote(ma2, ra2.at[i], s2a.at[i], q2a.at[i], zdev[i]) for i in range(3)]
    round2b = [
        remote(mb2.at[lax.select(y + i + 1 < 4, 1, 0)], rb2.at[i], s2b.at[i], q2b.at[i], ydev[i])
        for i in range(3)
    ]
    for i in range(3):
        round2b[i].start()
        pl.when(z + i + 1 < 4)(round2a[i].start)

    query(3)
    inside(1)

    w_on = []
    for i in range(3):
        w_piece[i].wait()
        source = ahead(x, 3 - i)
        for n in range(3):
            to = dev(
                lax.select(c == 0, z, ahead(z, n + 1)), lax.select(c == 0, ahead(y, n + 1), y), c, x
            )
            w_on.append(
                remote(
                    wof.at[source, pl.ds(at_piece, share)], wof.at[source, pl.ds(at_piece, share)],
                    wsy.at[i, n], wqy.at[i, n], to,
                )
            )
    for copy in w_on:
        copy.start()

    inside(2)
    inside(3)

    for i in range(3):
        round2b[i].wait()
        pb[...] += rb2[i].astype(F32)
        pl.when(z + i + 1 < 4)(round2a[i].wait_send)

        @pl.when(z >= i + 1)
        def _():
            round2a[i].wait_recv()
            pa[...] += ra2[i].astype(F32)

    before = jnp.concatenate([pa[...], pb[...]], axis=2)
    here = run[pl.ds(first, 2)]
    ps[...] = jnp.where(c == 0, before + here, before).astype(BF)
    round3 = remote(ps, pf.at[pl.ds(first, 2)], s3, q3, partner)
    round3.start()
    pf[pl.ds(first, 2)] = jnp.where(c == 1, before + r0[...].astype(F32), before).astype(BF)
    round3.wait()

    exchange = []
    for o in (2, 1, 3, 0):
        j = ahead(x, o)
        rows = pl.ds(pl.multiple_of(j * CHUNK, CHUNK), CHUNK)
        for h in range(4):
            feat = qf[rows, h * 256 : (h + 1) * 256]
            total = acc[h, rows] + dot_nt(feat, widen(pf[h]))
            atts[o, :, h * 128 : (h + 1) * 128] = (total[:, :128] / total[:, 128:]).astype(BF)
        if o:
            copy = remote(atts.at[o], attb.at[o - 1], sA.at[o - 1], qA.at[o - 1], xdev[o - 1])
            copy.start()
            exchange.append((o, copy))

    loads[7].wait()

    for copy in w_on + w_direct:
        copy.wait()
    w_pair = []
    for i in range(3):
        rows = pl.ds(pl.multiple_of(half, 256), 256)
        source = ahead(x, 3 - i)
        w_pair.append(
            remote(wof.at[source, rows], wof.at[source, rows], wsp.at[i], wqp.at[i], partner)
        )
        w_pair[i].start()

    res[...] = dot(atts[0], wof[x])
    for i in range(3):
        w_pair[i].wait()
    for o, copy in sorted(exchange, key=lambda pair: -(pair[0] % 2)):
        copy.wait()
        res[...] += dot(attb[o - 1], wof[ahead(x, 4 - o)])
    out[...] = res[...].astype(BF)


def shards(tokens, w_query, w_key, w_value, omega, w_out):
    dma = pltpu.SemaphoreType.DMA
    state = (2, 128 + NORM, 256)
    part = (2, 128 + NORM, 128)
    anywhere = pl.BlockSpec(memory_space=pl.ANY)
    vmem = pl.BlockSpec(memory_space=pltpu.VMEM)
    V = pltpu.VMEM
    return pl.pallas_call(
        kernel,
        out_shape=jax.ShapeDtypeStruct((CHUNK, 2048), BF),
        in_specs=[anywhere, anywhere, anywhere, anywhere, vmem, anywhere],
        out_specs=vmem,
        scratch_shapes=[
            V((1024, 2048), BF), V((2048, 512), BF), V((2048, 512), BF), V((2048, 512), BF),
            V((4, 512, 2048), BF), V((1024, 1024), BF), V((1024, 1024), BF), V((1024, 512), BF),
            V((512, 256), BF), V((4, 128 + NORM, 256), F32), V((4, 4, 128 + NORM, 256), BF),
            V((4, 1024, 256), F32), V((CHUNK, 2048), F32),
            V(state, BF), V(state, BF),
            V(part, BF), V((3,) + part, BF), V(part, BF), V((3,) + part, BF),
            V(part, BF), V((3,) + part, BF), V((2,) + part, BF), V((3,) + part, BF),
            V(part, F32), V(part, F32), V(part, F32),
            V(state, BF), V((4, 128 + NORM, 256), BF),
            V((4, CHUNK, 512), BF), V((3, CHUNK, 512), BF),
            dma((8,)), dma(()), dma(()),
            dma((3,)), dma((3,)), dma((3,)), dma((3,)), dma((3,)), dma((3,)), dma((3,)), dma((3,)),
            dma(()), dma(()), dma((3,)), dma((3,)),
            dma((3,)), dma((3,)), dma((3,)), dma((3,)), dma((3, 3)), dma((3, 3)), dma((3,)), dma((3,)),
        ],
        compiler_params=pltpu.CompilerParams(
            collective_id=0, has_side_effects=True, vmem_limit_bytes=60 << 20
        ),
        name="causal_linear",
    )(tokens, w_query, w_key, w_value, omega, w_out)


def solution(mesh):
    placed = (
        P("seq", None), P(None, "head"), P(None, "head"), P(None, "head"), P(), P("head", None),
    )
    return jax.shard_map(
        shards, mesh=mesh, in_specs=placed, out_specs=P(("seq", "head"), None), check_vma=False
    )
```

```python
import jax
import jax.numpy as jnp
from jax import lax
from jax.experimental import pallas as pl
from jax.experimental.pallas import tpu as pltpu
from jax.sharding import PartitionSpec as P

MESH = pl.DeviceIdType.MESH
BF, F32 = jnp.bfloat16, jnp.float32
LOG2E = 1.4426950408889634
CHUNK = 256
GROUPS = 2
NH = 4 // GROUPS
PIECE = 64

NT = (((1,), (1,)), ((), ()))


def dot(a, b):
    return jnp.dot(a, b, preferred_element_type=F32)


def dot_nt(a, b):
    return lax.dot_general(a, b, NT, preferred_element_type=F32)


def kernel(
    tok, wq, wk, wv, om, wo, out,
    tokv, wqv, wkv, omv, wof, kf, qf, vv, omw, run, sloc, acc, res,
    r0, ma, ra, ma2, ra2, mb, rb, mb2, rb2, pa, ua, pb, ps, pf, pw, atts, attb,
    lsem, s0, q0, s1a, q1a, s1b, q1b, s2a, q2a, s2b, q2b, s3, q3, sA, qA,
    wsx, wqx, wsy, wqy, wsz, wqz, wsp, wqp,
):
    seq, x = lax.axis_index("seq"), lax.axis_index("head")
    z, y, c = lax.div(seq, 8), lax.rem(lax.div(seq, 2), 4), lax.rem(seq, 2)

    def ahead(v, o):
        return lax.rem(v + o, 4)

    def dev(z_, y_, c_, x_):
        return {"seq": z_ * 8 + y_ * 2 + c_, "head": x_}

    partner = dev(z, y, 1 - c, x)
    ydev = [dev(z, ahead(y, o), c, x) for o in (1, 2, 3)]
    zdev = [dev(ahead(z, o), y, c, x) for o in (1, 2, 3)]
    xdev = [dev(z, y, c, ahead(x, o)) for o in (1, 2, 3)]

    def remote(src, dst, ss, rs, to):
        return pltpu.make_async_remote_copy(
            src_ref=src, dst_ref=dst, send_sem=ss, recv_sem=rs, device_id=to, device_id_type=MESH
        )

    def load(src, dst, i):
        copy = pltpu.make_async_copy(src, dst, lsem.at[i])
        copy.start()
        return copy

    def rows_of(j):
        return pl.ds(j * CHUNK, CHUNK)

    load_om = load(om, omv, 0)
    load_tok, load_kv = [], []
    for j in range(4):
        load_tok.append(load(tok.at[rows_of(j)], tokv.at[rows_of(j)], 1 + j))
        if j == 0:
            for g in range(GROUPS):
                cols = pl.ds(g * NH * 128, NH * 128)
                load_kv.append(
                    (
                        load(wk.at[:, cols], wkv.at[g, :, pl.ds(0, NH * 128)], 5 + 2 * g),
                        load(wv.at[:, cols], wkv.at[g, :, pl.ds(NH * 128, NH * 128)], 6 + 2 * g),
                    )
                )
    load_q = load(wq, wqv, 13)
    load_o = load(wo, wof.at[x], 14)

    barrier = pltpu.get_barrier_semaphore()
    for to in [partner] + ydev + zdev + xdev:
        pl.semaphore_signal(barrier, inc=1, device_id=to, device_id_type=MESH)

    run[...] = jnp.zeros_like(run)
    load_om.wait()

    scale = 128.0**-0.25
    omega = omv[...] * (scale * LOG2E)
    om_hi = omega.astype(BF)
    om_lo = (omega - om_hi.astype(F32)).astype(BF)
    omw[pl.ds(0, 128)] = om_hi
    omw[pl.ds(128, 128)] = om_hi
    omw[pl.ds(256, 128)] = om_lo
    omw[pl.ds(384, 128)] = jnp.full((128, 256), -1.0, BF)

    low = lax.broadcasted_iota(jnp.int32, (CHUNK, 128), 1) < 64

    def features(p):
        hi = p.astype(BF)
        lo = (p - hi.astype(F32)).astype(BF)
        square = p * p * (0.5 * scale * scale * LOG2E)
        pair = square + pltpu.roll(square, 64, 1) + 4.0 / 64
        pair_hi = pair.astype(BF).astype(F32)
        sums = jnp.where(low, pair_hi, pair - pair_hi).astype(BF)
        power = dot(jnp.concatenate([hi, lo, hi, sums], axis=1), omw[...])
        return (jnp.exp2(power) + 0.001 / 16).astype(BF)

    pl.semaphore_wait(barrier, 10)

    half = c * 256
    mine = lax.select(c == 0, y, z)

    def piece(o, start=0, size=PIECE):
        return pl.ds(pl.multiple_of(half + ahead(mine, o) * PIECE + start, 32), size)

    def along(o):
        return dev(
            lax.select(c == 0, z, ahead(z, o)), lax.select(c == 0, ahead(y, o), y), c, x
        )

    ends = [along(1), along(3)]
    w_x, w_y, w_z, w_p = [], [], [], []
    for i in range(3):
        source = ahead(x, 3 - i)
        shard = wof.at[source]
        w_x.append(
            remote(wo.at[piece(0)], wof.at[x, piece(0)], wsx.at[i], wqx.at[i], xdev[i])
        )
        w_y.append(
            [remote(shard.at[piece(0)], shard.at[piece(0)], wsy.at[i, d], wqy.at[i, d], ends[d])
             for d in range(2)]
        )
        spans = [piece(3, 0, 32), piece(1, 32, 32)]
        w_z.append(
            [remote(shard.at[spans[d]], shard.at[spans[d]], wsz.at[i, d], wqz.at[i, d], ends[d])
             for d in range(2)]
        )
        spans = [piece(0), piece(3), piece(1), piece(2, 0, 32), piece(2, 32, 32)]
        w_p.append(
            [remote(shard.at[span], shard.at[span], wsp.at[i, n], wqp.at[i, n], partner)
             for n, span in enumerate(spans)]
        )
    for i in range(3):
        w_x[i].start()

    def w_first(i):
        w_x[i].wait_recv()
        w_y[i][0].start()
        w_y[i][1].start()
        w_p[i][0].start()

    def w_second(i):
        for d in range(2):
            w_y[i][d].wait_recv()
            w_z[i][d].start()
            w_p[i][1 + d].start()

    def w_third(i):
        for d in range(2):
            w_z[i][d].wait_recv()
            w_p[i][3 + d].start()

    def key_value(g, j):
        rows = rows_of(j)
        both = dot(tokv[rows], wkv[g])
        for i in range(NH):
            h = g * NH + i
            feat = features(both[:, i * 128 : (i + 1) * 128])
            v = both[:, (NH + i) * 128 : (NH + i + 1) * 128]
            kf[rows, h * 256 : (h + 1) * 256] = feat
            vv[rows, h * 128 : (h + 1) * 128] = v.astype(BF)
            turned = v.T.astype(BF)
            norm = jnp.ones((16, CHUNK), BF)
            state = dot(jnp.concatenate([turned[:64], norm, turned[64:], norm], axis=0), feat)
            for a in range(2):
                for l in range(2):
                    so_far = run[l, h, a]
                    sloc[j, h, a * 80 : a * 80 + 80, l * 128 : (l + 1) * 128] = so_far.astype(BF)
                    run[l, h, a] = so_far + state[a * 80 : a * 80 + 80, l * 128 : (l + 1) * 128]

    causal = lax.broadcasted_iota(jnp.int32, (CHUNK, CHUNK), 0) >= lax.broadcasted_iota(
        jnp.int32, (CHUNK, CHUNK), 1
    )
    ones = jnp.ones((CHUNK, 128), BF)

    def query(j):
        rows = rows_of(j)
        q = dot(tokv[rows], wqv[...])
        for h in range(4):
            qf[rows, h * 256 : (h + 1) * 256] = features(q[:, h * 128 : (h + 1) * 128])

    def inside(g, j):
        rows = rows_of(j)
        for h in range(g * NH, (g + 1) * NH):
            feat = qf[rows, h * 256 : (h + 1) * 256]
            scores = dot_nt(feat, kf[rows, h * 256 : (h + 1) * 256])
            weights = jnp.where(causal, scores, 0.0).astype(BF)
            value = jnp.concatenate([vv[rows, h * 128 : (h + 1) * 128], ones], axis=1)
            total = dot(weights, value)
            if j > 0:
                local = sloc[j, h]
                norm = local[64:80]
                total = total + dot_nt(
                    feat, jnp.concatenate([local[:64], local[80:144]] + [norm] * 8, axis=0)
                )
            acc[h, rows] = total

    def heads(g):
        return pl.ds(g * NH, NH)

    def round0(g):
        return remote(run.at[1 - c, heads(g)], r0.at[heads(g)], s0.at[g], q0.at[g], partner)

    def round1(g):
        return (
            [remote(ma.at[heads(g)], ra.at[i, heads(g)], s1a.at[g, i], q1a.at[g, i], ydev[i]) for i in range(3)],
            [remote(mb.at[heads(g)], rb.at[i, heads(g)], s1b.at[g, i], q1b.at[g, i], zdev[i]) for i in range(3)],
        )

    def round2(g):
        return (
            [remote(ma2.at[heads(g)], ra2.at[i, heads(g)], s2a.at[g, i], q2a.at[g, i], zdev[i]) for i in range(3)],
            [
                remote(
                    mb2.at[lax.select(y + i + 1 < 4, 1, 0), heads(g)], rb2.at[i, heads(g)],
                    s2b.at[g, i], q2b.at[g, i], ydev[i],
                )
                for i in range(3)
            ],
        )

    def round3(g):
        return remote(ps.at[heads(g)], pf.at[c, heads(g)], s3.at[g], q3.at[g], partner)

    def start1(g):
        hs = heads(g)
        round0(g).wait()
        chip = run[c, hs] + r0[hs]
        ua[hs] = chip[:, 0]
        ma[hs] = chip[:, 0].astype(BF)
        mb[hs] = chip[:, 1].astype(BF)
        over_y, over_z = round1(g)
        for i in range(3):
            over_y[i].start()
            pl.when(z + i + 1 < 4)(over_z[i].start)

    def start2(g):
        hs = heads(g)
        over_y, over_z = round1(g)
        pa[hs] = jnp.zeros((NH, 80, 128), F32)
        pb[hs] = jnp.zeros((NH, 80, 128), F32)
        for i in range(3):
            over_y[i].wait()
            got = ra[i, hs].astype(F32)
            ua[hs] += got
            pa[hs] += jnp.where(y >= i + 1, got, 0.0)
            pl.when(z + i + 1 < 4)(over_z[i].wait_send)

            @pl.when(z >= i + 1)
            def _():
                over_z[i].wait_recv()
                pb[hs] += rb[i, hs].astype(F32)

        ma2[hs] = ua[hs].astype(BF)
        mb2[0, hs] = pb[hs].astype(BF)
        mb2[1, hs] = (pb[hs] + mb[hs].astype(F32)).astype(BF)
        over_z, over_y = round2(g)
        for i in range(3):
            over_y[i].start()
            pl.when(z + i + 1 < 4)(over_z[i].start)

    def start3(g):
        hs = heads(g)
        over_z, over_y = round2(g)
        for i in range(3):
            over_y[i].wait()
            pb[hs] += rb2[i, hs].astype(F32)
            pl.when(z + i + 1 < 4)(over_z[i].wait_send)

            @pl.when(z >= i + 1)
            def _():
                over_z[i].wait_recv()
                pa[hs] += ra2[i, hs].astype(F32)

        for a, part in enumerate((pa, pb)):
            before = part[hs]
            ps[hs, a] = jnp.where(c == 0, before + run[c, hs, a], before).astype(BF)
            pf[c, hs, a] = jnp.where(c == 1, before + r0[hs, a], before).astype(BF)
        round3(g).start()

    def exchange(g, o):
        return remote(atts.at[o, g], attb.at[o - 1, g], sA.at[g, o - 1], qA.at[g, o - 1], xdev[o - 1])

    def combine(g):
        round3(g).wait()
        for h in range(g * NH, (g + 1) * NH):
            for l in range(2):
                norm = pf[l, h, 0, 64:80]
                pw[h, :, l * 128 : (l + 1) * 128] = jnp.concatenate(
                    [pf[l, h, 0, 0:64], pf[l, h, 1, 0:64]] + [norm] * 8, axis=0
                )
        for o in (2, 1, 3, 0):
            rows = pl.ds(pl.multiple_of(ahead(x, o) * CHUNK, CHUNK), CHUNK)
            for i in range(NH):
                h = g * NH + i
                total = acc[h, rows] + dot_nt(qf[rows, h * 256 : (h + 1) * 256], pw[h])
                atts[o, g, :, i * 128 : (i + 1) * 128] = (total[:, :128] / total[:, 128:]).astype(BF)
            if o:
                exchange(g, o).start()

    def project(g, o):
        source = ahead(x, 4 - o) if o else x
        att = attb[o - 1, g] if o else atts[0, g]
        return dot(att, wof[source, pl.ds(g * NH * 128, NH * 128)])

    for copy in load_kv[0]:
        copy.wait()
    for j in range(4):
        load_tok[j].wait()
        key_value(0, j)
    round0(0).start()
    for copy in load_kv[1]:
        copy.wait()
    key_value(1, 0)
    key_value(1, 1)
    start1(0)
    key_value(1, 2)
    key_value(1, 3)
    round0(1).start()
    load_q.wait()
    query(0)
    start1(1)
    w_first(0)
    w_first(2)
    query(1)
    start2(0)
    query(2)
    query(3)
    w_first(1)
    for j in range(4):
        inside(0, j)
    start2(1)
    w_second(0)
    w_second(2)
    start3(0)
    for j in range(4):
        inside(1, j)
    combine(0)
    load_o.wait()
    res[...] = project(0, 0)
    w_second(1)
    w_third(0)
    w_third(2)
    start3(1)
    combine(1)
    w_third(1)
    res[...] += project(1, 0)
    for i in (0, 2, 1):
        for copy in w_p[i]:
            copy.wait_recv()
        exchange(0, i + 1).wait()
        res[...] += project(0, i + 1)
    for i in (0, 2):
        exchange(1, i + 1).wait()
        res[...] += project(1, i + 1)
    exchange(1, 2).wait()
    out[...] = (res[...] + project(1, 2)).astype(BF)
    for i in range(3):
        for copy in [w_x[i]] + w_y[i] + w_z[i] + w_p[i]:
            copy.wait_send()


def shards(tokens, w_query, w_key, w_value, omega, w_out):
    dma = pltpu.SemaphoreType.DMA
    V = pltpu.VMEM
    part = (4, 80, 128)
    whole = (4, 2, 80, 128)
    return pl.pallas_call(
        kernel,
        out_shape=jax.ShapeDtypeStruct((CHUNK, 2048), BF),
        in_specs=[pl.BlockSpec(memory_space=pltpu.HBM)] * 6,
        out_specs=pl.BlockSpec(memory_space=pltpu.VMEM),
        scratch_shapes=[
            V((1024, 2048), BF), V((2048, 512), BF), V((GROUPS, 2048, NH * 256), BF), V((128, 256), F32),
            V((4, 512, 2048), BF), V((1024, 1024), BF), V((1024, 1024), BF), V((1024, 512), BF),
            V((512, 256), BF), V((2,) + whole, F32), V((4, 4, 160, 256), BF),
            V((4, 1024, 256), F32), V((CHUNK, 2048), F32),
            V(whole, F32), V(part, BF), V((3,) + part, BF), V(part, BF), V((3,) + part, BF),
            V(part, BF), V((3,) + part, BF), V((2,) + part, BF), V((3,) + part, BF),
            V(part, F32), V(part, F32), V(part, F32),
            V(whole, BF), V((2,) + whole, BF), V((4, 256, 256), BF),
            V((4, GROUPS, CHUNK, NH * 128), BF), V((3, GROUPS, CHUNK, NH * 128), BF),
            dma((15,)), dma((GROUPS,)), dma((GROUPS,)),
            dma((GROUPS, 3)), dma((GROUPS, 3)), dma((GROUPS, 3)), dma((GROUPS, 3)),
            dma((GROUPS, 3)), dma((GROUPS, 3)), dma((GROUPS, 3)), dma((GROUPS, 3)),
            dma((GROUPS,)), dma((GROUPS,)), dma((GROUPS, 3)), dma((GROUPS, 3)),
            dma((3,)), dma((3,)), dma((3, 2)), dma((3, 2)), dma((3, 2)), dma((3, 2)), dma((3, 5)), dma((3, 5)),
        ],
        compiler_params=pltpu.CompilerParams(
            collective_id=0, has_side_effects=True, vmem_limit_bytes=42 << 20
        ),
        name="causal_linear",
    )(*[pltpu.with_memory_space_constraint(a, pltpu.HBM) for a in (tokens, w_query, w_key, w_value, omega, w_out)])


def solution(mesh):
    placed = (
        P("seq", None), P(None, "head"), P(None, "head"), P(None, "head"), P(), P("head", None),
    )
    return jax.shard_map(
        shards, mesh=mesh, in_specs=placed, out_specs=P(("seq", "head"), None), check_vma=False
    )
```

```python
import jax
import jax.numpy as jnp
from jax import lax
from jax.experimental import pallas as pl
from jax.experimental.pallas import tpu as pltpu
from jax.sharding import PartitionSpec as P

MESH = pl.DeviceIdType.MESH
BF, F32 = jnp.bfloat16, jnp.float32
LOG2E = 1.4426950408889634
CHUNK = 256
GROUPS = 4
NH = 4 // GROUPS
DIRECT = 64
PIECE = (256 - DIRECT) // 4
HALF = (16, PIECE - 16) if PIECE % 32 else (PIECE // 2, PIECE // 2)

NT = (((1,), (1,)), ((), ()))


def dot(a, b):
    return jnp.dot(a, b, preferred_element_type=F32)


def dot_nt(a, b):
    return lax.dot_general(a, b, NT, preferred_element_type=F32)


def kernel(
    tok, wq, wk, wv, om, wo, out,
    tokv, wqv, wkv, omv, wof, kf, qf, vv, omw, run, sloc, acc, res,
    r0, ma, ra, ma2, ra2, mb, rb, mb2, rb2, pa, ua, pb, ps, pf, pw, atts, attb,
    lsem, s0, q0, s1a, q1a, s1b, q1b, s2a, q2a, s2b, q2b, s3, q3, sA, qA,
    wss, wqs, wsp, wqp,
):
    seq, x = lax.axis_index("seq"), lax.axis_index("head")
    z, y, c = lax.div(seq, 8), lax.rem(lax.div(seq, 2), 4), lax.rem(seq, 2)

    def ahead(v, o):
        return lax.rem(v + o, 4)

    def dev(z_, y_, c_, x_):
        return {"seq": z_ * 8 + y_ * 2 + c_, "head": x_}

    partner = dev(z, y, 1 - c, x)
    ydev = [dev(z, ahead(y, o), c, x) for o in (1, 2, 3)]
    zdev = [dev(ahead(z, o), y, c, x) for o in (1, 2, 3)]
    xdev = [dev(z, y, c, ahead(x, o)) for o in (1, 2, 3)]

    def remote(src, dst, ss, rs, to):
        return pltpu.make_async_remote_copy(
            src_ref=src, dst_ref=dst, send_sem=ss, recv_sem=rs, device_id=to, device_id_type=MESH
        )

    def load(src, dst, i):
        copy = pltpu.make_async_copy(src, dst, lsem.at[i])
        copy.start()
        return copy

    def rows_of(j):
        return pl.ds(j * CHUNK, CHUNK)

    load_om = load(om, omv, 0)
    load_tok, load_kv = [], []
    def load_group(g):
        cols = pl.ds(g * NH * 128, NH * 128)
        load_kv.append(
            (
                load(wk.at[:, cols], wkv.at[g, :, pl.ds(0, NH * 128)], 5 + 2 * g),
                load(wv.at[:, cols], wkv.at[g, :, pl.ds(NH * 128, NH * 128)], 6 + 2 * g),
            )
        )

    for j in range(4):
        load_tok.append(load(tok.at[rows_of(j)], tokv.at[rows_of(j)], 1 + j))
        if j == 0:
            load_group(0)
    load_q = []

    barrier = pltpu.get_barrier_semaphore()
    for to in [partner] + ydev + zdev + xdev:
        pl.semaphore_signal(barrier, inc=1, device_id=to, device_id_type=MESH)

    run[...] = jnp.zeros_like(run)
    for copy in [load_tok[0], *load_kv[0]]:
        copy.wait()
    held = [dot(tokv[rows_of(0)], wkv[0])]
    load_om.wait()

    scale = 128.0**-0.25
    omega = omv[...] * (scale * LOG2E)
    om_hi = omega.astype(BF)
    om_lo = (omega - om_hi.astype(F32)).astype(BF)
    omw[pl.ds(0, 128)] = om_hi
    omw[pl.ds(128, 128)] = om_hi
    omw[pl.ds(256, 128)] = om_lo
    omw[pl.ds(384, 128)] = jnp.full((128, 256), -1.0, BF)

    low = lax.broadcasted_iota(jnp.int32, (CHUNK, 128), 1) < 64

    def features(p):
        hi = p.astype(BF)
        lo = (p - hi.astype(F32)).astype(BF)
        square = p * p * (0.5 * scale * scale * LOG2E)
        pair = square + pltpu.roll(square, 64, 1) + 4.0 / 64
        pair_hi = pair.astype(BF).astype(F32)
        sums = jnp.where(low, pair_hi, pair - pair_hi).astype(BF)
        power = dot(jnp.concatenate([hi, lo, hi, sums], axis=1), omw[...])
        return (jnp.exp2(power) + 0.001 / 16).astype(BF)

    pl.semaphore_wait(barrier, 10)

    half = c * 256
    mine = lax.select(c == 0, y, z)

    def piece(o, start=0, size=PIECE):
        return pl.ds(pl.multiple_of(half + DIRECT + ahead(mine, o) * PIECE + start, 16), size)

    def along(o):
        return dev(
            lax.select(c == 0, z, ahead(z, o)), lax.select(c == 0, ahead(y, o), y), c, x
        )

    ends, sides = [along(1), along(3)], [xdev[0], xdev[2]]
    shard = [wof.at[ahead(x, o)] for o in (3, 1, 2)]
    direct = pl.ds(pl.multiple_of(half, 64), DIRECT)
    direct_parts = [pl.ds(pl.multiple_of(half + d * 32, 32), 32) for d in range(2)]
    piece_parts = [(0, HALF[0]), (HALF[0], HALF[1])]

    def passes(k, i, d, span, to, from_wo=False):
        where = wof.at[x, span] if from_wo else shard[i].at[span]
        return remote(wo.at[span] if from_wo else where, where, wss.at[k, i, d], wqs.at[k, i, d], to)

    w_x1 = [passes(0, 0, d, piece(0), sides[d], True) for d in range(2)]
    w_d1 = [passes(0, 1, d, direct, sides[d], True) for d in range(2)]
    w_x2 = [passes(1, d, 0, piece(0, *piece_parts[d]), sides[d]) for d in range(2)]
    w_d2 = [passes(1, d, 1, direct_parts[d], sides[d]) for d in range(2)]
    w_y = [[passes(2, i, d, piece(0), ends[d]) for d in range(2)] for i in range(3)]
    w_z = [[passes(3, i, d, piece(3 - 2 * d, *piece_parts[d]), ends[d]) for d in range(2)] for i in range(3)]
    w_p = [
        [
            remote(shard[i].at[span], shard[i].at[span], wsp.at[i, n], wqp.at[i, n], partner)
            for n, span in enumerate(
                [piece(0), piece(3), piece(1), piece(2, *piece_parts[0]), piece(2, *piece_parts[1]), direct]
            )
        ]
        for i in range(3)
    ]
    for copy in w_x1 + w_d1:
        copy.start()
    for g in range(1, GROUPS):
        load_group(g)

    def w_along_head(i):
        w_x1[i].wait_recv()
        w_x2[i].start()

    def w_along_head_direct(i):
        w_d1[i].wait_recv()
        w_d2[i].start()

    def w_first(i):
        if i == 2:
            for copy in w_x2:
                copy.wait_recv()
        w_y[i][0].start()
        w_y[i][1].start()

    def w_second(i):
        for d in range(2):
            w_y[i][d].wait_recv()
            w_z[i][d].start()
            w_p[i][1 + d].start()

    def w_third(i):
        for d in range(2):
            w_z[i][d].wait_recv()
            w_p[i][3 + d].start()

    def key_value(g, j, both):
        rows = rows_of(j)
        for i in range(NH):
            h = g * NH + i
            feat = features(both[:, i * 128 : (i + 1) * 128])
            v = both[:, (NH + i) * 128 : (NH + i + 1) * 128]
            kf[rows, h * 256 : (h + 1) * 256] = feat
            vv[rows, h * 128 : (h + 1) * 128] = v.astype(BF)
            turned = v.T.astype(BF)
            norm = jnp.ones((16, CHUNK), BF)
            state = dot(jnp.concatenate([turned[:64], norm, turned[64:], norm], axis=0), feat)
            for a in range(2):
                for l in range(2):
                    so_far = run[l, h, a]
                    sloc[j, h, a * 80 : a * 80 + 80, l * 128 : (l + 1) * 128] = so_far.astype(BF)
                    run[l, h, a] = so_far + state[a * 80 : a * 80 + 80, l * 128 : (l + 1) * 128]

    causal = lax.broadcasted_iota(jnp.int32, (CHUNK, CHUNK), 0) >= lax.broadcasted_iota(
        jnp.int32, (CHUNK, CHUNK), 1
    )
    ones = jnp.ones((CHUNK, 128), BF)

    def query(n, j, q):
        rows = rows_of(j)
        for i in range(2):
            h = n * 2 + i
            qf[rows, h * 256 : (h + 1) * 256] = features(q[:, i * 128 : (i + 1) * 128])

    def inside(g, j):
        rows = rows_of(j)
        for h in range(g * NH, (g + 1) * NH):
            feat = qf[rows, h * 256 : (h + 1) * 256]
            scores = dot_nt(feat, kf[rows, h * 256 : (h + 1) * 256])
            weights = jnp.where(causal, scores, 0.0).astype(BF)
            value = jnp.concatenate([vv[rows, h * 128 : (h + 1) * 128], ones], axis=1)
            total = dot(weights, value)
            if j > 0:
                local = sloc[j, h]
                norm = local[64:80]
                total = total + dot_nt(
                    feat, jnp.concatenate([local[:64], local[80:144]] + [norm] * 8, axis=0)
                )
            acc[h, rows] = total

    def heads(g):
        return pl.ds(g * NH, NH)

    def round0(g):
        return remote(run.at[1 - c, heads(g)], r0.at[heads(g)], s0.at[g], q0.at[g], partner)

    def round1(g):
        return (
            [remote(ma.at[heads(g)], ra.at[i, heads(g)], s1a.at[g, i], q1a.at[g, i], ydev[i]) for i in range(3)],
            [remote(mb.at[heads(g)], rb.at[i, heads(g)], s1b.at[g, i], q1b.at[g, i], zdev[i]) for i in range(3)],
        )

    def round2(g):
        return (
            [remote(ma2.at[heads(g)], ra2.at[i, heads(g)], s2a.at[g, i], q2a.at[g, i], zdev[i]) for i in range(3)],
            [
                remote(
                    mb2.at[lax.select(y + i + 1 < 4, 1, 0), heads(g)], rb2.at[i, heads(g)],
                    s2b.at[g, i], q2b.at[g, i], ydev[i],
                )
                for i in range(3)
            ],
        )

    def round3(g):
        return remote(ps.at[heads(g)], pf.at[c, heads(g)], s3.at[g], q3.at[g], partner)

    def start1(g):
        hs = heads(g)
        round0(g).wait()
        chip = run[c, hs] + r0[hs]
        ua[hs] = chip[:, 0]
        ma[hs] = chip[:, 0].astype(BF)
        mb[hs] = chip[:, 1].astype(BF)
        over_y, over_z = round1(g)
        for i in range(3):
            over_y[i].start()
            pl.when(z + i + 1 < 4)(over_z[i].start)

    def start2(g):
        hs = heads(g)
        over_y, over_z = round1(g)
        pa[hs] = jnp.zeros((NH, 80, 128), F32)
        pb[hs] = jnp.zeros((NH, 80, 128), F32)
        for i in range(3):
            over_y[i].wait()
            got = ra[i, hs].astype(F32)
            ua[hs] += got
            pa[hs] += jnp.where(y >= i + 1, got, 0.0)
            pl.when(z + i + 1 < 4)(over_z[i].wait_send)

            @pl.when(z >= i + 1)
            def _():
                over_z[i].wait_recv()
                pb[hs] += rb[i, hs].astype(F32)

        ma2[hs] = ua[hs].astype(BF)
        mb2[0, hs] = pb[hs].astype(BF)
        mb2[1, hs] = (pb[hs] + mb[hs].astype(F32)).astype(BF)
        over_z, over_y = round2(g)
        for i in range(3):
            over_y[i].start()
            pl.when(z + i + 1 < 4)(over_z[i].start)

    def start3(g):
        hs = heads(g)
        over_z, over_y = round2(g)
        for i in range(3):
            over_y[i].wait()
            pb[hs] += rb2[i, hs].astype(F32)
            pl.when(z + i + 1 < 4)(over_z[i].wait_send)

            @pl.when(z >= i + 1)
            def _():
                over_z[i].wait_recv()
                pa[hs] += ra2[i, hs].astype(F32)

        for a, part in enumerate((pa, pb)):
            before = part[hs]
            ps[hs, a] = jnp.where(c == 0, before + run[c, hs, a], before).astype(BF)
            pf[c, hs, a] = jnp.where(c == 1, before + r0[hs, a], before).astype(BF)
        round3(g).start()

    def exchange(g, o):
        return remote(atts.at[o, :, pl.ds(g * NH * 128, NH * 128)], attb.at[o - 1, :, pl.ds(g * NH * 128, NH * 128)], sA.at[g, o - 1], qA.at[g, o - 1], xdev[o - 1])

    def combine(g):
        round3(g).wait()
        for h in range(g * NH, (g + 1) * NH):
            for l in range(2):
                norm = pf[l, h, 0, 64:80]
                pw[h, :, l * 128 : (l + 1) * 128] = jnp.concatenate(
                    [pf[l, h, 0, 0:64], pf[l, h, 1, 0:64]] + [norm] * 8, axis=0
                )
        order = (2, 1, 3, 0)
        totals = []
        for o in order:
            rows = pl.ds(pl.multiple_of(ahead(x, o) * CHUNK, CHUNK), CHUNK)
            for h in range(g * NH, (g + 1) * NH):
                totals.append(acc[h, rows] + dot_nt(qf[rows, h * 256 : (h + 1) * 256], pw[h]))
        for o in order:
            for h in range(g * NH, (g + 1) * NH):
                total = totals.pop(0)
                atts[o, :, h * 128 : (h + 1) * 128] = (total[:, :128] / total[:, 128:]).astype(BF)
        for o in order[:3]:
            exchange(g, o).start()

    def project(o, start, stop):
        source = ahead(x, 4 - o) if o else x
        att = attb[o - 1, :, start:stop] if o else atts[0, :, start:stop]
        return dot(att, wof[source, start:stop])

    stages = [("kv", g, j) for g in range(GROUPS) for j in range(4)]
    stages += [("q", n, j) for n in range(2) for j in range(4)]

    def front(kind, g, j):
        return dot(tokv[rows_of(j)], wqv[g] if kind == "q" else wkv[g])

    def step(count=1):
        for _ in range(count):
            (kind, g, j), wide = stages.pop(0), held.pop(0)
            if stages:
                held.append(front(*stages[0]))
            (query if kind == "q" else key_value)(g, j, wide)

    def insides(g):
        for j in range(4):
            inside(g, j)

    for copy in load_tok[1:3]:
        copy.wait()
    step(2)
    for copy in [load_tok[3], *load_kv[1]]:
        copy.wait()
    step(2)
    round0(0).start()
    for n in range(2):
        load_q.append(load(wq.at[:, pl.ds(n * 256, 256)], wqv.at[n], 13 + n))
    load_o = load(wo, wof.at[x], 15)
    for g in range(2, GROUPS):
        for copy in load_kv[g]:
            copy.wait()
    step(2)
    start1(0)
    step(2)
    round0(1).start()
    step(2)
    start1(1)
    step(2)
    round0(2).start()
    w_along_head(0)
    w_along_head(1)
    step(2)
    start2(0)
    start1(2)
    load_q[0].wait()
    load_q[1].wait()
    step(2)
    round0(3).start()
    step(2)
    start2(1)
    start1(3)
    step(2)
    start3(0)
    insides(0)
    start2(2)
    w_along_head_direct(0)
    w_along_head_direct(1)
    combine(0)
    for i in range(2):
        w_first(i)
        w_p[i][0].start()
        w_p[i][5].start()
    insides(1)
    start3(1)
    start2(3)
    w_first(2)
    step(2)
    combine(1)
    step(2)
    w_p[2][0].start()
    insides(2)
    start3(2)
    insides(3)
    w_second(0)
    w_second(1)
    combine(2)
    start3(3)
    load_o.wait()
    res[...] = project(0, 0, 256)
    combine(3)
    w_second(2)
    for copy in w_d2:
        copy.wait_recv()
    w_p[2][5].start()
    w_third(0)
    w_third(1)
    res[...] += project(0, 256, 512)
    for i in range(3):
        o = (1, 3, 2)[i]
        if i == 0:
            w_third(2)
        for copy in w_p[i]:
            copy.wait_recv()
        for g in range(GROUPS):
            exchange(g, o).wait()
        if i < 2:
            res[...] += project(o, 0, 512)
    out[...] = (res[...] + project(2, 0, 512)).astype(BF)
    for copy in w_x1 + w_d1 + w_x2 + w_d2 + sum(w_y + w_z + w_p, []):
        copy.wait_send()


def shards(tokens, w_query, w_key, w_value, omega, w_out):
    dma = pltpu.SemaphoreType.DMA
    V = pltpu.VMEM
    part = (4, 80, 128)
    whole = (4, 2, 80, 128)
    return pl.pallas_call(
        kernel,
        out_shape=jax.ShapeDtypeStruct((CHUNK, 2048), BF),
        in_specs=[pl.BlockSpec(memory_space=pltpu.HBM)] * 6,
        out_specs=pl.BlockSpec(memory_space=pltpu.VMEM),
        scratch_shapes=[
            V((1024, 2048), BF), V((2, 2048, 256), BF), V((GROUPS, 2048, NH * 256), BF), V((128, 256), F32),
            V((4, 512, 2048), BF), V((1024, 1024), BF), V((1024, 1024), BF), V((1024, 512), BF),
            V((512, 256), BF), V((2,) + whole, F32), V((4, 4, 160, 256), BF),
            V((4, 1024, 256), F32), V((CHUNK, 2048), F32),
            V(whole, F32), V(part, BF), V((3,) + part, BF), V(part, BF), V((3,) + part, BF),
            V(part, BF), V((3,) + part, BF), V((2,) + part, BF), V((3,) + part, BF),
            V(part, F32), V(part, F32), V(part, F32),
            V(whole, BF), V((2,) + whole, BF), V((4, 256, 256), BF),
            V((4, CHUNK, 512), BF), V((3, CHUNK, 512), BF),
            dma((16,)), dma((GROUPS,)), dma((GROUPS,)),
            dma((GROUPS, 3)), dma((GROUPS, 3)), dma((GROUPS, 3)), dma((GROUPS, 3)),
            dma((GROUPS, 3)), dma((GROUPS, 3)), dma((GROUPS, 3)), dma((GROUPS, 3)),
            dma((GROUPS,)), dma((GROUPS,)), dma((GROUPS, 3)), dma((GROUPS, 3)),
            dma((4, 3, 2)), dma((4, 3, 2)), dma((3, 6)), dma((3, 6)),
        ],
        compiler_params=pltpu.CompilerParams(
            collective_id=0, has_side_effects=True, vmem_limit_bytes=42 << 20
        ),
        name="causal_linear",
    )(*[pltpu.with_memory_space_constraint(a, pltpu.HBM) for a in (tokens, w_query, w_key, w_value, omega, w_out)])


def solution(mesh):
    placed = (
        P("seq", None), P(None, "head"), P(None, "head"), P(None, "head"), P(), P("head", None),
    )
    return jax.shard_map(
        shards, mesh=mesh, in_specs=placed, out_specs=P(("seq", "head"), None), check_vma=False
    )
```

```python
import jax
import jax.numpy as jnp
from jax import lax
from jax.experimental import pallas as pl
from jax.experimental.pallas import tpu as pltpu
from jax.sharding import PartitionSpec as P

MESH = pl.DeviceIdType.MESH
BF, F32 = jnp.bfloat16, jnp.float32
LOG2E = 1.4426950408889634
CHUNK = 256
GROUPS = 4
NH = 4 // GROUPS
DIRECT = 64
PIECE = (256 - DIRECT) // 4
HALF = (16, PIECE - 16) if PIECE % 32 else (PIECE // 2, PIECE // 2)

NT = (((1,), (1,)), ((), ()))


def dot(a, b):
    return jnp.dot(a, b, preferred_element_type=F32)


def dot_nt(a, b):
    return lax.dot_general(a, b, NT, preferred_element_type=F32)


def kernel(
    tok, wq, wk, wv, om, wo, out,
    tokv, wqv, wkv, omv, wof, kf, qf, vv, omw, run, sloc, acc, res,
    r0, ma, ra, ma2, ra2, mb, rb, mb2, rb2, pa, ua, pb, ps, pf, pw, atts, attb,
    lsem, s0, q0, s1a, q1a, s1b, q1b, s2a, q2a, s2b, q2b, s3, q3, sA, qA,
    wss, wqs, wsp, wqp,
):
    seq, x = lax.axis_index("seq"), lax.axis_index("head")
    z, y, c = lax.div(seq, 8), lax.rem(lax.div(seq, 2), 4), lax.rem(seq, 2)

    def ahead(v, o):
        return lax.rem(v + o, 4)

    def dev(z_, y_, c_, x_):
        return {"seq": z_ * 8 + y_ * 2 + c_, "head": x_}

    partner = dev(z, y, 1 - c, x)
    ydev = [dev(z, ahead(y, o), c, x) for o in (1, 2, 3)]
    zdev = [dev(ahead(z, o), y, c, x) for o in (1, 2, 3)]
    xdev = [dev(z, y, c, ahead(x, o)) for o in (1, 2, 3)]

    def remote(src, dst, ss, rs, to):
        return pltpu.make_async_remote_copy(
            src_ref=src, dst_ref=dst, send_sem=ss, recv_sem=rs, device_id=to, device_id_type=MESH
        )

    def load(src, dst, i):
        copy = pltpu.make_async_copy(src, dst, lsem.at[i])
        copy.start()
        return copy

    def rows_of(j):
        return pl.ds(j * CHUNK, CHUNK)

    load_om = load(om, omv, 0)
    load_tok, load_kv = [], []
    def load_group(g):
        cols = pl.ds(g * NH * 128, NH * 128)
        load_kv.append(
            (
                load(wk.at[:, cols], wkv.at[g, :, pl.ds(0, NH * 128)], 5 + 2 * g),
                load(wv.at[:, cols], wkv.at[g, :, pl.ds(NH * 128, NH * 128)], 6 + 2 * g),
            )
        )

    for j in range(4):
        load_tok.append(load(tok.at[rows_of(j)], tokv.at[rows_of(j)], 1 + j))
        if j == 0:
            load_group(0)
    load_q = []

    barrier = pltpu.get_barrier_semaphore()
    for to in [partner] + ydev + zdev + xdev:
        pl.semaphore_signal(barrier, inc=1, device_id=to, device_id_type=MESH)

    run[...] = jnp.zeros_like(run)
    for copy in [load_tok[0], *load_kv[0]]:
        copy.wait()
    held = [dot(tokv[rows_of(0)], wkv[0])]
    load_om.wait()

    scale = 128.0**-0.25
    omega = omv[...] * (scale * LOG2E)
    om_hi = omega.astype(BF)
    om_lo = (omega - om_hi.astype(F32)).astype(BF)
    omw[pl.ds(0, 128)] = om_hi
    omw[pl.ds(128, 128)] = om_hi
    omw[pl.ds(256, 128)] = om_lo
    omw[pl.ds(384, 128)] = jnp.full((128, 256), -1.0, BF)

    low = lax.broadcasted_iota(jnp.int32, (CHUNK, 128), 1) < 64

    def features(p):
        hi = p.astype(BF)
        lo = (p - hi.astype(F32)).astype(BF)
        square = p * p * (0.5 * scale * scale * LOG2E)
        pair = square + pltpu.roll(square, 64, 1) + 4.0 / 64
        pair_hi = pair.astype(BF).astype(F32)
        sums = jnp.where(low, pair_hi, pair - pair_hi).astype(BF)
        power = dot(jnp.concatenate([hi, lo, hi, sums], axis=1), omw[...])
        return (jnp.exp2(power) + 0.001 / 16).astype(BF)

    pl.semaphore_wait(barrier, 10)

    half = c * 256
    mine = lax.select(c == 0, y, z)

    def piece(o, start=0, size=PIECE):
        return pl.ds(pl.multiple_of(half + DIRECT + ahead(mine, o) * PIECE + start, 16), size)

    def along(o):
        return dev(
            lax.select(c == 0, z, ahead(z, o)), lax.select(c == 0, ahead(y, o), y), c, x
        )

    ends, sides = [along(1), along(3)], [xdev[0], xdev[2]]
    shard = [wof.at[ahead(x, o)] for o in (3, 1, 2)]
    direct = pl.ds(pl.multiple_of(half, 64), DIRECT)
    direct_parts = [pl.ds(pl.multiple_of(half + d * 32, 32), 32) for d in range(2)]
    piece_parts = [(0, HALF[0]), (HALF[0], HALF[1])]

    def passes(k, i, d, span, to, from_wo=False):
        where = wof.at[x, span] if from_wo else shard[i].at[span]
        return remote(wo.at[span] if from_wo else where, where, wss.at[k, i, d], wqs.at[k, i, d], to)

    w_x1 = [passes(0, 0, d, piece(0), sides[d], True) for d in range(2)]
    w_d1 = [passes(0, 1, d, direct, sides[d], True) for d in range(2)]
    w_x2 = [passes(1, d, 0, piece(0, *piece_parts[d]), sides[d]) for d in range(2)]
    w_d2 = [passes(1, d, 1, direct_parts[d], sides[d]) for d in range(2)]
    w_y = [[passes(2, i, d, piece(0), ends[d]) for d in range(2)] for i in range(3)]
    w_z = [[passes(3, i, d, piece(3 - 2 * d, *piece_parts[d]), ends[d]) for d in range(2)] for i in range(3)]
    w_p = [
        [
            remote(shard[i].at[span], shard[i].at[span], wsp.at[i, n], wqp.at[i, n], partner)
            for n, span in enumerate(
                [piece(0), piece(3), piece(1), piece(2, *piece_parts[0]), piece(2, *piece_parts[1]), direct]
            )
        ]
        for i in range(3)
    ]
    for copy in w_x1 + w_d1:
        copy.start()
    for g in range(1, GROUPS):
        load_group(g)

    def w_along_head(i):
        w_x1[i].wait_recv()
        w_x2[i].start()

    def w_along_head_direct(i):
        w_d1[i].wait_recv()
        w_d2[i].start()

    def w_first(i):
        if i == 2:
            for copy in w_x2:
                copy.wait_recv()
        w_y[i][0].start()
        w_y[i][1].start()

    def w_second(i):
        for d in range(2):
            w_y[i][d].wait_recv()
            w_z[i][d].start()
            w_p[i][1 + d].start()

    def w_third(i):
        for d in range(2):
            w_z[i][d].wait_recv()
            w_p[i][3 + d].start()

    def key_value(g, j, both):
        rows = rows_of(j)
        for i in range(NH):
            h = g * NH + i
            feat = features(both[:, i * 128 : (i + 1) * 128])
            v = both[:, (NH + i) * 128 : (NH + i + 1) * 128]
            kf[rows, h * 256 : (h + 1) * 256] = feat
            vv[rows, h * 128 : (h + 1) * 128] = v.astype(BF)
            turned = v.T.astype(BF)
            norm = jnp.ones((16, CHUNK), BF)
            state = dot(jnp.concatenate([turned[:64], norm, turned[64:], norm], axis=0), feat)
            for a in range(2):
                for l in range(2):
                    so_far = run[l, h, a]
                    sloc[j, h, a * 80 : a * 80 + 80, l * 128 : (l + 1) * 128] = so_far.astype(BF)
                    run[l, h, a] = so_far + state[a * 80 : a * 80 + 80, l * 128 : (l + 1) * 128]

    causal = lax.broadcasted_iota(jnp.int32, (CHUNK, CHUNK), 0) >= lax.broadcasted_iota(
        jnp.int32, (CHUNK, CHUNK), 1
    )
    ones = jnp.ones((CHUNK, 128), BF)

    def query(n, j, q):
        rows = rows_of(j)
        for i in range(2):
            h = n * 2 + i
            qf[rows, h * 256 : (h + 1) * 256] = features(q[:, i * 128 : (i + 1) * 128])

    def inside(g, j):
        rows = rows_of(j)
        for h in range(g * NH, (g + 1) * NH):
            feat = qf[rows, h * 256 : (h + 1) * 256]
            scores = dot_nt(feat, kf[rows, h * 256 : (h + 1) * 256])
            weights = jnp.where(causal, scores, 0.0).astype(BF)
            value = jnp.concatenate([vv[rows, h * 128 : (h + 1) * 128], ones], axis=1)
            total = dot(weights, value)
            if j > 0:
                local = sloc[j, h]
                norm = local[64:80]
                total = total + dot_nt(
                    feat, jnp.concatenate([local[:64], local[80:144]] + [norm] * 8, axis=0)
                )
            acc[h, rows] = total

    def heads(g):
        return pl.ds(g * NH, NH)

    def round0(g):
        return remote(run.at[1 - c, heads(g)], r0.at[heads(g)], s0.at[g], q0.at[g], partner)

    def round1(g):
        return (
            [remote(ma.at[heads(g)], ra.at[i, heads(g)], s1a.at[g, i], q1a.at[g, i], ydev[i]) for i in range(3)],
            [remote(mb.at[heads(g)], rb.at[i, heads(g)], s1b.at[g, i], q1b.at[g, i], zdev[i]) for i in range(3)],
        )

    def round2(g):
        return (
            [remote(ma2.at[heads(g)], ra2.at[i, heads(g)], s2a.at[g, i], q2a.at[g, i], zdev[i]) for i in range(3)],
            [
                remote(
                    mb2.at[lax.select(y + i + 1 < 4, 1, 0), heads(g)], rb2.at[i, heads(g)],
                    s2b.at[g, i], q2b.at[g, i], ydev[i],
                )
                for i in range(3)
            ],
        )

    def round3(g):
        return remote(ps.at[heads(g)], pf.at[c, heads(g)], s3.at[g], q3.at[g], partner)

    def start1(g):
        hs = heads(g)
        round0(g).wait()
        chip = run[c, hs] + r0[hs]
        ua[hs] = chip[:, 0]
        ma[hs] = chip[:, 0].astype(BF)
        mb[hs] = chip[:, 1].astype(BF)
        over_y, over_z = round1(g)
        for i in range(3):
            over_y[i].start()
            pl.when(z + i + 1 < 4)(over_z[i].start)

    def start2(g):
        hs = heads(g)
        over_y, over_z = round1(g)
        pa[hs] = jnp.zeros((NH, 80, 128), F32)
        pb[hs] = jnp.zeros((NH, 80, 128), F32)
        for i in range(3):
            over_y[i].wait()
            got = ra[i, hs].astype(F32)
            ua[hs] += got
            pa[hs] += jnp.where(y >= i + 1, got, 0.0)
            pl.when(z + i + 1 < 4)(over_z[i].wait_send)

            @pl.when(z >= i + 1)
            def _():
                over_z[i].wait_recv()
                pb[hs] += rb[i, hs].astype(F32)

        ma2[hs] = ua[hs].astype(BF)
        mb2[0, hs] = pb[hs].astype(BF)
        mb2[1, hs] = (pb[hs] + mb[hs].astype(F32)).astype(BF)
        over_z, over_y = round2(g)
        for i in range(3):
            over_y[i].start()
            pl.when(z + i + 1 < 4)(over_z[i].start)

    def start3(g):
        hs = heads(g)
        over_z, over_y = round2(g)
        for i in range(3):
            over_y[i].wait()
            pb[hs] += rb2[i, hs].astype(F32)
            pl.when(z + i + 1 < 4)(over_z[i].wait_send)

            @pl.when(z >= i + 1)
            def _():
                over_z[i].wait_recv()
                pa[hs] += ra2[i, hs].astype(F32)

        for a, part in enumerate((pa, pb)):
            before = part[hs]
            ps[hs, a] = jnp.where(c == 0, before + run[c, hs, a], before).astype(BF)
            pf[c, hs, a] = jnp.where(c == 1, before + r0[hs, a], before).astype(BF)
        round3(g).start()

    def exchange(g, o):
        return remote(atts.at[o, :, pl.ds(g * NH * 128, NH * 128)], attb.at[o - 1, :, pl.ds(g * NH * 128, NH * 128)], sA.at[g, o - 1], qA.at[g, o - 1], xdev[o - 1])

    def combine(g):
        round3(g).wait()
        for h in range(g * NH, (g + 1) * NH):
            for l in range(2):
                norm = pf[l, h, 0, 64:80]
                pw[h, :, l * 128 : (l + 1) * 128] = jnp.concatenate(
                    [pf[l, h, 0, 0:64], pf[l, h, 1, 0:64]] + [norm] * 8, axis=0
                )
        order = (2, 1, 3, 0)
        totals = []
        for o in order:
            rows = pl.ds(pl.multiple_of(ahead(x, o) * CHUNK, CHUNK), CHUNK)
            for h in range(g * NH, (g + 1) * NH):
                totals.append(acc[h, rows] + dot_nt(qf[rows, h * 256 : (h + 1) * 256], pw[h]))
        for o in order:
            for h in range(g * NH, (g + 1) * NH):
                total = totals.pop(0)
                atts[o, :, h * 128 : (h + 1) * 128] = (total[:, :128] / total[:, 128:]).astype(BF)
        for o in order[:3]:
            exchange(g, o).start()

    def project(o, start, stop):
        source = ahead(x, 4 - o) if o else x
        att = attb[o - 1, :, start:stop] if o else atts[0, :, start:stop]
        return dot(att, wof[source, start:stop])

    stages = [("kv", g, j) for g in range(GROUPS) for j in range(4)]
    stages += [("q", n, j) for n in range(2) for j in range(4)]

    def front(kind, g, j):
        return dot(tokv[rows_of(j)], wqv[g] if kind == "q" else wkv[g])

    def step(count=1):
        for _ in range(count):
            (kind, g, j), wide = stages.pop(0), held.pop(0)
            if stages:
                held.append(front(*stages[0]))
            (query if kind == "q" else key_value)(g, j, wide)

    def insides(g):
        for j in range(4):
            inside(g, j)

    for copy in load_tok[1:3]:
        copy.wait()
    step(2)
    for copy in [load_tok[3], *load_kv[1]]:
        copy.wait()
    step(2)
    round0(0).start()
    for n in range(2):
        load_q.append(load(wq.at[:, pl.ds(n * 256, 256)], wqv.at[n], 13 + n))
    load_o = load(wo, wof.at[x], 15)
    for g in range(2, GROUPS):
        for copy in load_kv[g]:
            copy.wait()
    step(2)
    start1(0)
    step(2)
    round0(1).start()
    step(2)
    start1(1)
    step(2)
    round0(2).start()
    w_along_head(0)
    w_along_head(1)
    step(2)
    start2(0)
    start1(2)
    load_q[0].wait()
    load_q[1].wait()
    step(2)
    round0(3).start()
    step(2)
    start2(1)
    start1(3)
    step(2)
    w_first(0)
    start3(0)
    insides(0)
    start2(2)
    w_along_head_direct(0)
    w_along_head_direct(1)
    combine(0)
    w_first(1)
    insides(1)
    start3(1)
    start2(3)
    step(2)
    w_first(2)
    combine(1)
    for i in range(2):
        w_p[i][0].start()
        w_p[i][5].start()
    step(2)
    w_second(0)
    insides(2)
    start3(2)
    insides(3)
    combine(2)
    start3(3)
    load_o.wait()
    res[...] = project(0, 0, 256)
    w_p[2][0].start()
    w_second(1)
    combine(3)
    w_second(2)
    for copy in w_d2:
        copy.wait_recv()
    w_p[2][5].start()
    w_third(0)
    res[...] += project(0, 256, 512)
    w_third(1)
    for i in range(3):
        o = (1, 3, 2)[i]
        if i == 1:
            w_third(2)
        for copy in w_p[i]:
            copy.wait_recv()
        for g in range(2):
            exchange(g, o).wait()
        res[...] += project(o, 0, 256)
    for o in (1, 3, 2):
        for g in range(2, 4):
            exchange(g, o).wait()
        if o != 2:
            res[...] += project(o, 256, 512)
    out[...] = (res[...] + project(2, 256, 512)).astype(BF)
    for copy in w_x1 + w_d1 + w_x2 + w_d2 + sum(w_y + w_z + w_p, []):
        copy.wait_send()


def shards(tokens, w_query, w_key, w_value, omega, w_out):
    dma = pltpu.SemaphoreType.DMA
    V = pltpu.VMEM
    part = (4, 80, 128)
    whole = (4, 2, 80, 128)
    return pl.pallas_call(
        kernel,
        out_shape=jax.ShapeDtypeStruct((CHUNK, 2048), BF),
        in_specs=[pl.BlockSpec(memory_space=pltpu.HBM)] * 6,
        out_specs=pl.BlockSpec(memory_space=pltpu.VMEM),
        scratch_shapes=[
            V((1024, 2048), BF), V((2, 2048, 256), BF), V((GROUPS, 2048, NH * 256), BF), V((128, 256), F32),
            V((4, 512, 2048), BF), V((1024, 1024), BF), V((1024, 1024), BF), V((1024, 512), BF),
            V((512, 256), BF), V((2,) + whole, F32), V((4, 4, 160, 256), BF),
            V((4, 1024, 256), F32), V((CHUNK, 2048), F32),
            V(whole, F32), V(part, BF), V((3,) + part, BF), V(part, BF), V((3,) + part, BF),
            V(part, BF), V((3,) + part, BF), V((2,) + part, BF), V((3,) + part, BF),
            V(part, F32), V(part, F32), V(part, F32),
            V(whole, BF), V((2,) + whole, BF), V((4, 256, 256), BF),
            V((4, CHUNK, 512), BF), V((3, CHUNK, 512), BF),
            dma((16,)), dma((GROUPS,)), dma((GROUPS,)),
            dma((GROUPS, 3)), dma((GROUPS, 3)), dma((GROUPS, 3)), dma((GROUPS, 3)),
            dma((GROUPS, 3)), dma((GROUPS, 3)), dma((GROUPS, 3)), dma((GROUPS, 3)),
            dma((GROUPS,)), dma((GROUPS,)), dma((GROUPS, 3)), dma((GROUPS, 3)),
            dma((4, 3, 2)), dma((4, 3, 2)), dma((3, 6)), dma((3, 6)),
        ],
        compiler_params=pltpu.CompilerParams(
            collective_id=0, has_side_effects=True, vmem_limit_bytes=42 << 20
        ),
        name="causal_linear",
    )(*[pltpu.with_memory_space_constraint(a, pltpu.HBM) for a in (tokens, w_query, w_key, w_value, omega, w_out)])


def solution(mesh):
    placed = (
        P("seq", None), P(None, "head"), P(None, "head"), P(None, "head"), P(), P("head", None),
    )
    return jax.shard_map(
        shards, mesh=mesh, in_specs=placed, out_specs=P(("seq", "head"), None), check_vma=False
    )
```

```python
import jax
import jax.numpy as jnp
from jax import lax
from jax.experimental import pallas as pl
from jax.experimental.pallas import tpu as pltpu
from jax.sharding import PartitionSpec as P

MESH = pl.DeviceIdType.MESH
BF, F32 = jnp.bfloat16, jnp.float32
LOG2E = 1.4426950408889634
CHUNK = 256
GROUPS = 4
NH = 4 // GROUPS
DIRECT = 64
PIECE = (256 - DIRECT) // 4
HALF = (16, PIECE - 16) if PIECE % 32 else (PIECE // 2, PIECE // 2)

NT = (((1,), (1,)), ((), ()))


def dot(a, b):
    return jnp.dot(a, b, preferred_element_type=F32)


def dot_nt(a, b):
    return lax.dot_general(a, b, NT, preferred_element_type=F32)


def kernel(
    tok, wq, wk, wv, om, wo, out,
    tokv, wqv, wkv, omv, wof, kf, qf, vv, omw, run, sloc, acc, res,
    r0, ma, ra, ma2, ra2, mb, rb, mb2, rb2, pa, ua, pb, ps, pf, pw, atts, attb,
    lsem, s0, q0, s1a, q1a, s1b, q1b, s2a, q2a, s2b, q2b, s3, q3, sA, qA,
    wss, wqs, wsp, wqp,
):
    seq, x = lax.axis_index("seq"), lax.axis_index("head")
    z, y, c = lax.div(seq, 8), lax.rem(lax.div(seq, 2), 4), lax.rem(seq, 2)

    def ahead(v, o):
        return lax.rem(v + o, 4)

    def dev(z_, y_, c_, x_):
        return {"seq": z_ * 8 + y_ * 2 + c_, "head": x_}

    partner = dev(z, y, 1 - c, x)
    ydev = [dev(z, ahead(y, o), c, x) for o in (1, 2, 3)]
    zdev = [dev(ahead(z, o), y, c, x) for o in (1, 2, 3)]
    xdev = [dev(z, y, c, ahead(x, o)) for o in (1, 2, 3)]

    def remote(src, dst, ss, rs, to):
        return pltpu.make_async_remote_copy(
            src_ref=src, dst_ref=dst, send_sem=ss, recv_sem=rs, device_id=to, device_id_type=MESH
        )

    def load(src, dst, i):
        copy = pltpu.make_async_copy(src, dst, lsem.at[i])
        copy.start()
        return copy

    def rows_of(j):
        return pl.ds(j * CHUNK, CHUNK)

    load_om = load(om, omv, 0)
    load_tok, load_kv = [], []
    def load_group(g):
        cols = pl.ds(g * NH * 128, NH * 128)
        load_kv.append(
            (
                load(wk.at[:, cols], wkv.at[g, :, pl.ds(0, NH * 128)], 5 + 2 * g),
                load(wv.at[:, cols], wkv.at[g, :, pl.ds(NH * 128, NH * 128)], 6 + 2 * g),
            )
        )

    load_tok.append(load(tok.at[rows_of(0)], tokv.at[rows_of(0)], 1))
    load_group(0)
    for j in range(1, 4):
        load_tok.append(load(tok.at[rows_of(j)], tokv.at[rows_of(j)], 1 + j))
    load_q = []

    barrier = pltpu.get_barrier_semaphore()
    for to in [partner] + ydev + zdev + xdev:
        pl.semaphore_signal(barrier, inc=1, device_id=to, device_id_type=MESH)

    for copy in [load_tok[0], *load_kv[0]]:
        copy.wait()
    held = [dot(tokv[rows_of(0)], wkv[0])]
    load_om.wait()

    scale = 128.0**-0.25
    omega = omv[...] * (scale * LOG2E)
    om_hi = omega.astype(BF)
    om_lo = (omega - om_hi.astype(F32)).astype(BF)
    omw[pl.ds(0, 128)] = om_hi
    omw[pl.ds(128, 128)] = om_hi
    omw[pl.ds(256, 128)] = om_lo
    omw[pl.ds(384, 128)] = jnp.full((128, 256), -1.0, BF)

    low = lax.broadcasted_iota(jnp.int32, (CHUNK, 128), 1) < 64

    def features(p):
        hi = p.astype(BF)
        lo = (p - hi.astype(F32)).astype(BF)
        square = p * p * (0.5 * scale * scale * LOG2E)
        pair = square + pltpu.roll(square, 64, 1) + 4.0 / 64
        pair_hi = pair.astype(BF).astype(F32)
        sums = jnp.where(low, pair_hi, pair - pair_hi).astype(BF)
        power = dot(jnp.concatenate([hi, lo, hi, sums], axis=1), omw[...])
        return (jnp.exp2(power) + 0.001 / 16).astype(BF)

    pl.semaphore_wait(barrier, 10)

    half = c * 256
    mine = lax.select(c == 0, y, z)

    def piece(o, start=0, size=PIECE):
        return pl.ds(pl.multiple_of(half + DIRECT + ahead(mine, o) * PIECE + start, 16), size)

    def along(o):
        return dev(
            lax.select(c == 0, z, ahead(z, o)), lax.select(c == 0, ahead(y, o), y), c, x
        )

    ends, sides = [along(1), along(3)], [xdev[0], xdev[2]]
    shard = [wof.at[ahead(x, o)] for o in (3, 1, 2)]
    direct = pl.ds(pl.multiple_of(half, 64), DIRECT)
    direct_parts = [pl.ds(pl.multiple_of(half + d * 32, 32), 32) for d in range(2)]
    piece_parts = [(0, HALF[0]), (HALF[0], HALF[1])]

    def passes(k, i, d, span, to, from_wo=False):
        where = wof.at[x, span] if from_wo else shard[i].at[span]
        return remote(wo.at[span] if from_wo else where, where, wss.at[k, i, d], wqs.at[k, i, d], to)

    w_x1 = [passes(0, 0, d, piece(0), sides[d], True) for d in range(2)]
    w_d1 = [passes(0, 1, d, direct, sides[d], True) for d in range(2)]
    w_x2 = [passes(1, d, 0, piece(0, *piece_parts[d]), sides[d]) for d in range(2)]
    w_d2 = [passes(1, d, 1, direct_parts[d], sides[d]) for d in range(2)]
    w_y = [[passes(2, i, d, piece(0), ends[d]) for d in range(2)] for i in range(3)]
    w_z = [[passes(3, i, d, piece(3 - 2 * d, *piece_parts[d]), ends[d]) for d in range(2)] for i in range(3)]
    w_p = [
        [
            remote(shard[i].at[span], shard[i].at[span], wsp.at[i, n], wqp.at[i, n], partner)
            for n, span in enumerate(
                [piece(0), piece(3), piece(1), piece(2, *piece_parts[0]), piece(2, *piece_parts[1]), direct]
            )
        ]
        for i in range(3)
    ]
    for copy in w_x1 + w_d1:
        copy.start()
    for g in range(1, GROUPS):
        load_group(g)

    def w_along_head(i):
        w_x1[i].wait_recv()
        w_x2[i].start()

    def w_along_head_direct(i):
        w_d1[i].wait_recv()
        w_d2[i].start()

    def w_first(i):
        if i == 2:
            for copy in w_x2:
                copy.wait_recv()
        w_y[i][0].start()
        w_y[i][1].start()

    def w_second(i):
        for d in range(2):
            w_y[i][d].wait_recv()
            w_z[i][d].start()
            w_p[i][1 + d].start()

    def w_third(i):
        for d in range(2):
            w_z[i][d].wait_recv()
            w_p[i][3 + d].start()

    def key_value(g, j, both):
        rows = rows_of(j)
        for i in range(NH):
            h = g * NH + i
            feat = features(both[:, i * 128 : (i + 1) * 128])
            v = both[:, (NH + i) * 128 : (NH + i + 1) * 128]
            kf[rows, h * 256 : (h + 1) * 256] = feat
            vv[rows, h * 128 : (h + 1) * 128] = v.astype(BF)
            turned = v.T.astype(BF)
            norm = jnp.ones((16, CHUNK), BF)
            state = dot(jnp.concatenate([turned[:64], norm, turned[64:], norm], axis=0), feat)
            for a in range(2):
                for l in range(2):
                    part = state[a * 80 : a * 80 + 80, l * 128 : (l + 1) * 128]
                    if j > 0:
                        so_far = run[l, h, a]
                        sloc[j, h, a * 80 : a * 80 + 80, l * 128 : (l + 1) * 128] = so_far.astype(BF)
                        part = so_far + part
                    run[l, h, a] = part

    causal = lax.broadcasted_iota(jnp.int32, (CHUNK, CHUNK), 0) >= lax.broadcasted_iota(
        jnp.int32, (CHUNK, CHUNK), 1
    )
    ones = jnp.ones((CHUNK, 128), BF)

    def query(n, j, q):
        rows = rows_of(j)
        for i in range(2):
            h = n * 2 + i
            qf[rows, h * 256 : (h + 1) * 256] = features(q[:, i * 128 : (i + 1) * 128])

    def inside(g, j):
        rows = rows_of(j)
        for h in range(g * NH, (g + 1) * NH):
            feat = qf[rows, h * 256 : (h + 1) * 256]
            scores = dot_nt(feat, kf[rows, h * 256 : (h + 1) * 256])
            weights = jnp.where(causal, scores, 0.0).astype(BF)
            value = jnp.concatenate([vv[rows, h * 128 : (h + 1) * 128], ones], axis=1)
            total = dot(weights, value)
            if j > 0:
                local = sloc[j, h]
                norm = local[64:80]
                total = total + dot_nt(
                    feat, jnp.concatenate([local[:64], local[80:144]] + [norm] * 8, axis=0)
                )
            acc[h, rows] = total

    def heads(g):
        return pl.ds(g * NH, NH)

    def round0(g):
        return remote(run.at[1 - c, heads(g)], r0.at[heads(g)], s0.at[g], q0.at[g], partner)

    def round1(g):
        return (
            [remote(ma.at[heads(g)], ra.at[i, heads(g)], s1a.at[g, i], q1a.at[g, i], ydev[i]) for i in range(3)],
            [remote(mb.at[heads(g)], rb.at[i, heads(g)], s1b.at[g, i], q1b.at[g, i], zdev[i]) for i in range(3)],
        )

    def round2(g):
        return (
            [remote(ma2.at[heads(g)], ra2.at[i, heads(g)], s2a.at[g, i], q2a.at[g, i], zdev[i]) for i in range(3)],
            [
                remote(
                    mb2.at[lax.select(y + i + 1 < 4, 1, 0), heads(g)], rb2.at[i, heads(g)],
                    s2b.at[g, i], q2b.at[g, i], ydev[i],
                )
                for i in range(3)
            ],
        )

    def round3(g):
        return remote(ps.at[heads(g)], pf.at[c, heads(g)], s3.at[g], q3.at[g], partner)

    def start1(g):
        hs = heads(g)
        round0(g).wait()
        chip = run[c, hs] + r0[hs]
        ua[hs] = chip[:, 0]
        ma[hs] = chip[:, 0].astype(BF)
        mb[hs] = chip[:, 1].astype(BF)
        over_y, over_z = round1(g)
        for i in range(3):
            over_y[i].start()
            pl.when(z + i + 1 < 4)(over_z[i].start)

    def start2(g):
        hs = heads(g)
        over_y, over_z = round1(g)
        pa[hs] = jnp.zeros((NH, 80, 128), F32)
        pb[hs] = jnp.zeros((NH, 80, 128), F32)
        for i in range(3):
            over_y[i].wait()
            got = ra[i, hs].astype(F32)
            ua[hs] += got
            pa[hs] += jnp.where(y >= i + 1, got, 0.0)
            pl.when(z + i + 1 < 4)(over_z[i].wait_send)

            @pl.when(z >= i + 1)
            def _():
                over_z[i].wait_recv()
                pb[hs] += rb[i, hs].astype(F32)

        ma2[hs] = ua[hs].astype(BF)
        mb2[0, hs] = pb[hs].astype(BF)
        mb2[1, hs] = (pb[hs] + mb[hs].astype(F32)).astype(BF)
        over_z, over_y = round2(g)
        for i in range(3):
            over_y[i].start()
            pl.when(z + i + 1 < 4)(over_z[i].start)

    def start3(g):
        hs = heads(g)
        over_z, over_y = round2(g)
        for i in range(3):
            over_y[i].wait()
            pb[hs] += rb2[i, hs].astype(F32)
            pl.when(z + i + 1 < 4)(over_z[i].wait_send)

            @pl.when(z >= i + 1)
            def _():
                over_z[i].wait_recv()
                pa[hs] += ra2[i, hs].astype(F32)

        for a, part in enumerate((pa, pb)):
            before = part[hs]
            ps[hs, a] = jnp.where(c == 0, before + run[c, hs, a], before).astype(BF)
            pf[c, hs, a] = jnp.where(c == 1, before + r0[hs, a], before).astype(BF)
        round3(g).start()

    def exchange(g, o):
        return remote(atts.at[o, :, pl.ds(g * NH * 128, NH * 128)], attb.at[o - 1, :, pl.ds(g * NH * 128, NH * 128)], sA.at[g, o - 1], qA.at[g, o - 1], xdev[o - 1])

    def combine(g):
        round3(g).wait()
        for h in range(g * NH, (g + 1) * NH):
            for l in range(2):
                norm = pf[l, h, 0, 64:80]
                pw[h, :, l * 128 : (l + 1) * 128] = jnp.concatenate(
                    [pf[l, h, 0, 0:64], pf[l, h, 1, 0:64]] + [norm] * 8, axis=0
                )
        order = (2, 1, 3, 0)
        totals = []
        for o in order:
            rows = pl.ds(pl.multiple_of(ahead(x, o) * CHUNK, CHUNK), CHUNK)
            for h in range(g * NH, (g + 1) * NH):
                totals.append(acc[h, rows] + dot_nt(qf[rows, h * 256 : (h + 1) * 256], pw[h]))
        for o in order:
            for h in range(g * NH, (g + 1) * NH):
                total = totals.pop(0)
                atts[o, :, h * 128 : (h + 1) * 128] = (total[:, :128] / total[:, 128:]).astype(BF)
        for o in order[:3]:
            exchange(g, o).start()

    def project(o, start, stop):
        source = ahead(x, 4 - o) if o else x
        att = attb[o - 1, :, start:stop] if o else atts[0, :, start:stop]
        return dot(att, wof[source, start:stop])

    stages = [("kv", g, j) for g in range(GROUPS) for j in range(4)]
    stages += [("q", n, j) for n in range(2) for j in range(4)]

    def front(kind, g, j):
        return dot(tokv[rows_of(j)], wqv[g] if kind == "q" else wkv[g])

    def step(count=1):
        for _ in range(count):
            (kind, g, j), wide = stages.pop(0), held.pop(0)
            if stages:
                held.append(front(*stages[0]))
            (query if kind == "q" else key_value)(g, j, wide)

    def insides(g):
        for j in range(4):
            inside(g, j)

    for copy in load_tok[1:3]:
        copy.wait()
    step(2)
    for copy in [load_tok[3], *load_kv[1]]:
        copy.wait()
    step(2)
    round0(0).start()
    for n in range(2):
        load_q.append(load(wq.at[:, pl.ds(n * 256, 256)], wqv.at[n], 13 + n))
    load_o = load(wo, wof.at[x], 15)
    for g in range(2, GROUPS):
        for copy in load_kv[g]:
            copy.wait()
    step(2)
    start1(0)
    step(2)
    round0(1).start()
    step(2)
    start1(1)
    step(2)
    round0(2).start()
    w_along_head(0)
    w_along_head(1)
    step(2)
    start2(0)
    start1(2)
    load_q[0].wait()
    load_q[1].wait()
    step(2)
    round0(3).start()
    step(2)
    start2(1)
    start1(3)
    step(2)
    w_first(0)
    start3(0)
    insides(0)
    start2(2)
    w_along_head_direct(0)
    w_along_head_direct(1)
    combine(0)
    w_first(1)
    insides(1)
    start3(1)
    start2(3)
    step(2)
    w_first(2)
    combine(1)
    for i in range(2):
        w_p[i][0].start()
        w_p[i][5].start()
    step(2)
    w_second(0)
    insides(2)
    start3(2)
    insides(3)
    combine(2)
    start3(3)
    load_o.wait()
    res[...] = project(0, 0, 256)
    w_p[2][0].start()
    w_second(1)
    combine(3)
    w_second(2)
    for copy in w_d2:
        copy.wait_recv()
    w_p[2][5].start()
    w_third(0)
    res[...] += project(0, 256, 512)
    w_third(1)
    for i in range(3):
        o = (1, 3, 2)[i]
        if i == 1:
            w_third(2)
        for copy in w_p[i]:
            copy.wait_recv()
        for g in range(2):
            exchange(g, o).wait()
        res[...] += project(o, 0, 256)
    for o in (1, 3, 2):
        for g in range(2, 4):
            exchange(g, o).wait()
        if o != 2:
            res[...] += project(o, 256, 512)
    out[...] = (res[...] + project(2, 256, 512)).astype(BF)
    for copy in w_x1 + w_d1 + w_x2 + w_d2 + sum(w_y + w_z + w_p, []):
        copy.wait_send()


def shards(tokens, w_query, w_key, w_value, omega, w_out):
    dma = pltpu.SemaphoreType.DMA
    V = pltpu.VMEM
    part = (4, 80, 128)
    whole = (4, 2, 80, 128)
    return pl.pallas_call(
        kernel,
        out_shape=jax.ShapeDtypeStruct((CHUNK, 2048), BF),
        in_specs=[pl.BlockSpec(memory_space=pltpu.HBM)] * 6,
        out_specs=pl.BlockSpec(memory_space=pltpu.VMEM),
        scratch_shapes=[
            V((1024, 2048), BF), V((2, 2048, 256), BF), V((GROUPS, 2048, NH * 256), BF), V((128, 256), F32),
            V((4, 512, 2048), BF), V((1024, 1024), BF), V((1024, 1024), BF), V((1024, 512), BF),
            V((512, 256), BF), V((2,) + whole, F32), V((4, 4, 160, 256), BF),
            V((4, 1024, 256), F32), V((CHUNK, 2048), F32),
            V(whole, F32), V(part, BF), V((3,) + part, BF), V(part, BF), V((3,) + part, BF),
            V(part, BF), V((3,) + part, BF), V((2,) + part, BF), V((3,) + part, BF),
            V(part, F32), V(part, F32), V(part, F32),
            V(whole, BF), V((2,) + whole, BF), V((4, 256, 256), BF),
            V((4, CHUNK, 512), BF), V((3, CHUNK, 512), BF),
            dma((16,)), dma((GROUPS,)), dma((GROUPS,)),
            dma((GROUPS, 3)), dma((GROUPS, 3)), dma((GROUPS, 3)), dma((GROUPS, 3)),
            dma((GROUPS, 3)), dma((GROUPS, 3)), dma((GROUPS, 3)), dma((GROUPS, 3)),
            dma((GROUPS,)), dma((GROUPS,)), dma((GROUPS, 3)), dma((GROUPS, 3)),
            dma((4, 3, 2)), dma((4, 3, 2)), dma((3, 6)), dma((3, 6)),
        ],
        compiler_params=pltpu.CompilerParams(
            collective_id=0, has_side_effects=True, vmem_limit_bytes=42 << 20
        ),
        name="causal_linear",
    )(*[pltpu.with_memory_space_constraint(a, pltpu.HBM) for a in (tokens, w_query, w_key, w_value, omega, w_out)])


def solution(mesh):
    placed = (
        P("seq", None), P(None, "head"), P(None, "head"), P(None, "head"), P(), P("head", None),
    )
    return jax.shard_map(
        shards, mesh=mesh, in_specs=placed, out_specs=P(("seq", "head"), None), check_vma=False
    )
```

```python
import jax
import jax.numpy as jnp
from jax import lax
from jax.experimental import pallas as pl
from jax.experimental.pallas import tpu as pltpu
from jax.sharding import PartitionSpec as P

MESH = pl.DeviceIdType.MESH
BF, F32 = jnp.bfloat16, jnp.float32
LOG2E = 1.4426950408889634
CHUNK = 256
GROUPS = 4
NH = 4 // GROUPS
DIRECT = 64
PIECE = (256 - DIRECT) // 4
HALF = (16, PIECE - 16) if PIECE % 32 else (PIECE // 2, PIECE // 2)

NT = (((1,), (1,)), ((), ()))


def dot(a, b):
    return jnp.dot(a, b, preferred_element_type=F32)


def dot_nt(a, b):
    return lax.dot_general(a, b, NT, preferred_element_type=F32)


def kernel(
    tok, wq, wk, wv, om, wo, out,
    tokv, wqv, wkv, omv, wof, kf, qf, vv, omw, run, sloc, acc, res,
    r0, ma, ra, ma2, ra2, mb, rb, mb2, rb2, pa, ua, pb, ps, pf, pw, atts, attb,
    lsem, s0, q0, s1a, q1a, s1b, q1b, s2a, q2a, s2b, q2b, s3, q3, sA, qA,
    wss, wqs, wsp, wqp,
):
    seq, x = lax.axis_index("seq"), lax.axis_index("head")
    z, y, c = lax.div(seq, 8), lax.rem(lax.div(seq, 2), 4), lax.rem(seq, 2)

    def ahead(v, o):
        return lax.rem(v + o, 4)

    def dev(z_, y_, c_, x_):
        return {"seq": z_ * 8 + y_ * 2 + c_, "head": x_}

    partner = dev(z, y, 1 - c, x)
    ydev = [dev(z, ahead(y, o), c, x) for o in (1, 2, 3)]
    zdev = [dev(ahead(z, o), y, c, x) for o in (1, 2, 3)]
    xdev = [dev(z, y, c, ahead(x, o)) for o in (1, 2, 3)]

    def remote(src, dst, ss, rs, to):
        return pltpu.make_async_remote_copy(
            src_ref=src, dst_ref=dst, send_sem=ss, recv_sem=rs, device_id=to, device_id_type=MESH
        )

    def load(src, dst, i):
        copy = pltpu.make_async_copy(src, dst, lsem.at[i])
        copy.start()
        return copy

    def rows_of(j):
        return pl.ds(j * CHUNK, CHUNK)

    load_om = load(om, omv, 0)
    load_tok, load_kv = [], []
    def load_group(g):
        cols = pl.ds(g * NH * 128, NH * 128)
        load_kv.append(
            (
                load(wk.at[:, cols], wkv.at[g, :, pl.ds(0, NH * 128)], 5 + 2 * g),
                load(wv.at[:, cols], wkv.at[g, :, pl.ds(NH * 128, NH * 128)], 6 + 2 * g),
            )
        )

    load_tok.append(load(tok.at[rows_of(0)], tokv.at[rows_of(0)], 1))
    load_group(0)
    for j in range(1, 4):
        load_tok.append(load(tok.at[rows_of(j)], tokv.at[rows_of(j)], 1 + j))
    load_q = []

    barrier = pltpu.get_barrier_semaphore()
    for to in [partner] + ydev + zdev + xdev:
        pl.semaphore_signal(barrier, inc=1, device_id=to, device_id_type=MESH)

    for copy in [load_tok[0], *load_kv[0]]:
        copy.wait()
    held = [dot(tokv[rows_of(0)], wkv[0])]
    load_om.wait()

    scale = 128.0**-0.25
    omega = omv[...] * (scale * LOG2E)
    om_hi = omega.astype(BF)
    om_lo = (omega - om_hi.astype(F32)).astype(BF)
    omw[pl.ds(0, 128)] = om_hi
    omw[pl.ds(128, 128)] = om_hi
    omw[pl.ds(256, 128)] = om_lo
    omw[pl.ds(384, 128)] = jnp.full((128, 256), -1.0, BF)

    low = lax.broadcasted_iota(jnp.int32, (CHUNK, 128), 1) < 64

    def features(p):
        hi = p.astype(BF)
        lo = (p - hi.astype(F32)).astype(BF)
        square = p * p * (0.5 * scale * scale * LOG2E)
        pair = square + pltpu.roll(square, 64, 1) + 4.0 / 64
        pair_hi = pair.astype(BF).astype(F32)
        sums = jnp.where(low, pair_hi, pair - pair_hi).astype(BF)
        power = dot(jnp.concatenate([hi, lo, hi, sums], axis=1), omw[...])
        return (jnp.exp2(power) + 0.001 / 16).astype(BF)

    pl.semaphore_wait(barrier, 10)

    half = c * 256
    mine = lax.select(c == 0, y, z)

    def piece(o, start=0, size=PIECE):
        return pl.ds(pl.multiple_of(half + DIRECT + ahead(mine, o) * PIECE + start, 16), size)

    def along(o):
        return dev(
            lax.select(c == 0, z, ahead(z, o)), lax.select(c == 0, ahead(y, o), y), c, x
        )

    ends, sides = [along(1), along(3)], [xdev[0], xdev[2]]
    shard = [wof.at[ahead(x, o)] for o in (3, 1, 2)]
    direct = pl.ds(pl.multiple_of(half, 64), DIRECT)
    direct_parts = [pl.ds(pl.multiple_of(half + d * 32, 32), 32) for d in range(2)]
    piece_parts = [(0, HALF[0]), (HALF[0], HALF[1])]

    def passes(k, i, d, span, to, from_wo=False):
        where = wof.at[x, span] if from_wo else shard[i].at[span]
        return remote(wo.at[span] if from_wo else where, where, wss.at[k, i, d], wqs.at[k, i, d], to)

    w_x1 = [passes(0, 0, d, piece(0), sides[d], True) for d in range(2)]
    w_d1 = [passes(0, 1, d, direct, sides[d], True) for d in range(2)]
    w_x2 = [passes(1, d, 0, piece(0, *piece_parts[d]), sides[d]) for d in range(2)]
    w_d2 = [passes(1, d, 1, direct_parts[d], sides[d]) for d in range(2)]
    w_y = [[passes(2, i, d, piece(0), ends[d]) for d in range(2)] for i in range(3)]
    w_z = [[passes(3, i, d, piece(3 - 2 * d, *piece_parts[d]), ends[d]) for d in range(2)] for i in range(3)]
    w_p = [
        [
            remote(shard[i].at[span], shard[i].at[span], wsp.at[i, n], wqp.at[i, n], partner)
            for n, span in enumerate(
                [piece(0), piece(3), piece(1), piece(2, *piece_parts[0]), piece(2, *piece_parts[1]), direct]
            )
        ]
        for i in range(3)
    ]
    for copy in w_x1 + w_d1:
        copy.start()
    for g in range(1, GROUPS):
        load_group(g)

    def w_along_head(i):
        w_x1[i].wait_recv()
        w_x2[i].start()

    def w_along_head_direct(i):
        w_d1[i].wait_recv()
        w_d2[i].start()

    def w_first(i):
        if i == 2:
            for copy in w_x2:
                copy.wait_recv()
        w_y[i][0].start()
        w_y[i][1].start()

    def w_second(i):
        for d in range(2):
            w_y[i][d].wait_recv()
            w_z[i][d].start()
            w_p[i][1 + d].start()

    def w_third(i):
        for d in range(2):
            w_z[i][d].wait_recv()
            w_p[i][3 + d].start()

    def key_value(g, j, both):
        rows = rows_of(j)
        for i in range(NH):
            h = g * NH + i
            feat = features(both[:, i * 128 : (i + 1) * 128])
            v = both[:, (NH + i) * 128 : (NH + i + 1) * 128]
            kf[rows, h * 256 : (h + 1) * 256] = feat
            vv[rows, h * 128 : (h + 1) * 128] = v.astype(BF)
            turned = v.T.astype(BF)
            norm = jnp.ones((16, CHUNK), BF)
            state = dot(jnp.concatenate([turned[:64], norm, turned[64:], norm], axis=0), feat)
            for a in range(2):
                for l in range(2):
                    part = state[a * 80 : a * 80 + 80, l * 128 : (l + 1) * 128]
                    if j > 0:
                        so_far = run[l, h, a]
                        sloc[j, h, a * 80 : a * 80 + 80, l * 128 : (l + 1) * 128] = so_far.astype(BF)
                        part = so_far + part
                    run[l, h, a] = part

    causal = lax.broadcasted_iota(jnp.int32, (CHUNK, CHUNK), 0) >= lax.broadcasted_iota(
        jnp.int32, (CHUNK, CHUNK), 1
    )
    ones = jnp.ones((CHUNK, 128), BF)

    def query(n, j, q):
        rows = rows_of(j)
        for i in range(2):
            h = n * 2 + i
            qf[rows, h * 256 : (h + 1) * 256] = features(q[:, i * 128 : (i + 1) * 128])

    def inside(g, j):
        rows = rows_of(j)
        for h in range(g * NH, (g + 1) * NH):
            feat = qf[rows, h * 256 : (h + 1) * 256]
            scores = dot_nt(feat, kf[rows, h * 256 : (h + 1) * 256])
            weights = jnp.where(causal, scores, 0.0).astype(BF)
            value = jnp.concatenate([vv[rows, h * 128 : (h + 1) * 128], ones], axis=1)
            total = dot(weights, value)
            if j > 0:
                local = sloc[j, h]
                norm = local[64:80]
                total = total + dot_nt(
                    feat, jnp.concatenate([local[:64], local[80:144]] + [norm] * 8, axis=0)
                )
            acc[h, rows] = total

    def heads(g):
        return pl.ds(g * NH, NH)

    def round0(g):
        return remote(run.at[1 - c, heads(g)], r0.at[heads(g)], s0.at[g], q0.at[g], partner)

    def round1(g):
        return (
            [remote(ma.at[heads(g)], ra.at[i, heads(g)], s1a.at[g, i], q1a.at[g, i], ydev[i]) for i in range(3)],
            [remote(mb.at[heads(g)], rb.at[i, heads(g)], s1b.at[g, i], q1b.at[g, i], zdev[i]) for i in range(3)],
        )

    def round2(g):
        return (
            [remote(ma2.at[heads(g)], ra2.at[i, heads(g)], s2a.at[g, i], q2a.at[g, i], zdev[i]) for i in range(3)],
            [
                remote(
                    mb2.at[lax.select(y + i + 1 < 4, 1, 0), heads(g)], rb2.at[i, heads(g)],
                    s2b.at[g, i], q2b.at[g, i], ydev[i],
                )
                for i in range(3)
            ],
        )

    def round3(g):
        return remote(ps.at[heads(g)], pf.at[c, heads(g)], s3.at[g], q3.at[g], partner)

    def start1(g):
        hs = heads(g)
        round0(g).wait()
        chip = run[c, hs] + r0[hs]
        ua[hs] = chip[:, 0]
        ma[hs] = chip[:, 0].astype(BF)
        mb[hs] = chip[:, 1].astype(BF)
        over_y, over_z = round1(g)
        for i in range(3):
            over_y[i].start()
            pl.when(z + i + 1 < 4)(over_z[i].start)

    def start2(g):
        hs = heads(g)
        over_y, over_z = round1(g)
        pa[hs] = jnp.zeros((NH, 80, 128), F32)
        pb[hs] = jnp.zeros((NH, 80, 128), F32)
        for i in range(3):
            over_y[i].wait()
            got = ra[i, hs].astype(F32)
            ua[hs] += got
            pa[hs] += jnp.where(y >= i + 1, got, 0.0)
            pl.when(z + i + 1 < 4)(over_z[i].wait_send)

            @pl.when(z >= i + 1)
            def _():
                over_z[i].wait_recv()
                pb[hs] += rb[i, hs].astype(F32)

        ma2[hs] = ua[hs].astype(BF)
        mb2[0, hs] = pb[hs].astype(BF)
        mb2[1, hs] = (pb[hs] + mb[hs].astype(F32)).astype(BF)
        over_z, over_y = round2(g)
        for i in range(3):
            over_y[i].start()
            pl.when(z + i + 1 < 4)(over_z[i].start)

    def start3(g):
        hs = heads(g)
        over_z, over_y = round2(g)
        for i in range(3):
            over_y[i].wait()
            pb[hs] += rb2[i, hs].astype(F32)
            pl.when(z + i + 1 < 4)(over_z[i].wait_send)

            @pl.when(z >= i + 1)
            def _():
                over_z[i].wait_recv()
                pa[hs] += ra2[i, hs].astype(F32)

        for a, part in enumerate((pa, pb)):
            before = part[hs]
            ps[hs, a] = jnp.where(c == 0, before + run[c, hs, a], before).astype(BF)
            pf[c, hs, a] = jnp.where(c == 1, before + r0[hs, a], before).astype(BF)
        round3(g).start()

    def exchange(g, o):
        return remote(atts.at[o, :, pl.ds(g * NH * 128, NH * 128)], attb.at[o - 1, :, pl.ds(g * NH * 128, NH * 128)], sA.at[g, o - 1], qA.at[g, o - 1], xdev[o - 1])

    def combine(g):
        round3(g).wait()
        for h in range(g * NH, (g + 1) * NH):
            for l in range(2):
                norm = pf[l, h, 0, 64:80]
                pw[h, :, l * 128 : (l + 1) * 128] = jnp.concatenate(
                    [pf[l, h, 0, 0:64], pf[l, h, 1, 0:64]] + [norm] * 8, axis=0
                )
        order = (2, 1, 3, 0)
        totals = []
        for o in order:
            rows = pl.ds(pl.multiple_of(ahead(x, o) * CHUNK, CHUNK), CHUNK)
            for h in range(g * NH, (g + 1) * NH):
                totals.append(acc[h, rows] + dot_nt(qf[rows, h * 256 : (h + 1) * 256], pw[h]))
        for o in order:
            for h in range(g * NH, (g + 1) * NH):
                total = totals.pop(0)
                atts[o, :, h * 128 : (h + 1) * 128] = (total[:, :128] / total[:, 128:]).astype(BF)
        for o in order[:3]:
            exchange(g, o).start()

    def project(o, start, stop):
        source = ahead(x, 4 - o) if o else x
        att = attb[o - 1, :, start:stop] if o else atts[0, :, start:stop]
        return dot(att, wof[source, start:stop])

    stages = [("kv", g, j) for g in range(GROUPS) for j in range(4)]
    stages += [("q", n, j) for n in range(2) for j in range(4)]

    def front(kind, g, j):
        return dot(tokv[rows_of(j)], wqv[g] if kind == "q" else wkv[g])

    def step(count=1):
        for _ in range(count):
            (kind, g, j), wide = stages.pop(0), held.pop(0)
            if stages:
                held.append(front(*stages[0]))
            (query if kind == "q" else key_value)(g, j, wide)

    def insides(g):
        for j in range(4):
            inside(g, j)

    for copy in load_tok[1:3]:
        copy.wait()
    step(2)
    for copy in [load_tok[3], *load_kv[1]]:
        copy.wait()
    step(2)
    round0(0).start()
    for n in range(2):
        load_q.append(load(wq.at[:, pl.ds(n * 256, 256)], wqv.at[n], 13 + n))
    load_o = load(wo, wof.at[x], 15)
    for g in range(2, GROUPS):
        for copy in load_kv[g]:
            copy.wait()
    step(2)
    start1(0)
    step(2)
    round0(1).start()
    step(2)
    start1(1)
    step(2)
    round0(2).start()
    w_along_head(0)
    w_along_head(1)
    step(2)
    start2(0)
    start1(2)
    load_q[0].wait()
    load_q[1].wait()
    step(2)
    round0(3).start()
    step(2)
    start2(1)
    start1(3)
    step(2)
    w_first(0)
    start3(0)
    w_along_head_direct(0)
    w_along_head_direct(1)
    insides(0)
    start2(2)
    combine(0)
    w_first(1)
    insides(1)
    start3(1)
    start2(3)
    step(2)
    w_first(2)
    combine(1)
    for i in range(2):
        w_p[i][0].start()
        w_p[i][5].start()
    step(2)
    w_second(0)
    insides(2)
    start3(2)
    insides(3)
    combine(2)
    start3(3)
    load_o.wait()
    res[...] = project(0, 0, 256)
    w_p[2][0].start()
    w_second(1)
    combine(3)
    w_second(2)
    for copy in w_d2:
        copy.wait_recv()
    w_p[2][5].start()
    w_third(0)
    res[...] += project(0, 256, 512)
    w_third(1)
    for i in range(3):
        o = (1, 3, 2)[i]
        if i == 1:
            w_third(2)
        for copy in w_p[i]:
            copy.wait_recv()
        for g in range(2):
            exchange(g, o).wait()
        if i < 2:
            res[...] += project(o, 0, 256)
        if i == 1:
            for near in (1, 3):
                for g in range(2, 4):
                    exchange(g, near).wait()
                res[...] += project(near, 256, 512)
    for g in range(2, 4):
        exchange(g, 2).wait()
    out[...] = (res[...] + project(2, 0, 512)).astype(BF)
    for copy in w_x1 + w_d1 + w_x2 + w_d2 + sum(w_y + w_z + w_p, []):
        copy.wait_send()


def shards(tokens, w_query, w_key, w_value, omega, w_out):
    dma = pltpu.SemaphoreType.DMA
    V = pltpu.VMEM
    part = (4, 80, 128)
    whole = (4, 2, 80, 128)
    return pl.pallas_call(
        kernel,
        out_shape=jax.ShapeDtypeStruct((CHUNK, 2048), BF),
        in_specs=[pl.BlockSpec(memory_space=pltpu.HBM)] * 6,
        out_specs=pl.BlockSpec(memory_space=pltpu.VMEM),
        scratch_shapes=[
            V((1024, 2048), BF), V((2, 2048, 256), BF), V((GROUPS, 2048, NH * 256), BF), V((128, 256), F32),
            V((4, 512, 2048), BF), V((1024, 1024), BF), V((1024, 1024), BF), V((1024, 512), BF),
            V((512, 256), BF), V((2,) + whole, F32), V((4, 4, 160, 256), BF),
            V((4, 1024, 256), F32), V((CHUNK, 2048), F32),
            V(whole, F32), V(part, BF), V((3,) + part, BF), V(part, BF), V((3,) + part, BF),
            V(part, BF), V((3,) + part, BF), V((2,) + part, BF), V((3,) + part, BF),
            V(part, F32), V(part, F32), V(part, F32),
            V(whole, BF), V((2,) + whole, BF), V((4, 256, 256), BF),
            V((4, CHUNK, 512), BF), V((3, CHUNK, 512), BF),
            dma((16,)), dma((GROUPS,)), dma((GROUPS,)),
            dma((GROUPS, 3)), dma((GROUPS, 3)), dma((GROUPS, 3)), dma((GROUPS, 3)),
            dma((GROUPS, 3)), dma((GROUPS, 3)), dma((GROUPS, 3)), dma((GROUPS, 3)),
            dma((GROUPS,)), dma((GROUPS,)), dma((GROUPS, 3)), dma((GROUPS, 3)),
            dma((4, 3, 2)), dma((4, 3, 2)), dma((3, 6)), dma((3, 6)),
        ],
        compiler_params=pltpu.CompilerParams(
            collective_id=0, has_side_effects=True, vmem_limit_bytes=42 << 20
        ),
        name="causal_linear",
    )(*[pltpu.with_memory_space_constraint(a, pltpu.HBM) for a in (tokens, w_query, w_key, w_value, omega, w_out)])


def solution(mesh):
    placed = (
        P("seq", None), P(None, "head"), P(None, "head"), P(None, "head"), P(), P("head", None),
    )
    return jax.shard_map(
        shards, mesh=mesh, in_specs=placed, out_specs=P(("seq", "head"), None), check_vma=False
    )
```

```python
import jax
import jax.numpy as jnp
from jax import lax
from jax.experimental import pallas as pl
from jax.experimental.pallas import tpu as pltpu
from jax.sharding import PartitionSpec as P

MESH = pl.DeviceIdType.MESH
BF, F32 = jnp.bfloat16, jnp.float32
LOG2E = 1.4426950408889634
CHUNK = 256
GROUPS = 4
NH = 4 // GROUPS
DIRECT = 64
PIECE = (256 - DIRECT) // 4
HALF = (16, PIECE - 16) if PIECE % 32 else (PIECE // 2, PIECE // 2)

NT = (((1,), (1,)), ((), ()))


def dot(a, b):
    return jnp.dot(a, b, preferred_element_type=F32)


def dot_nt(a, b):
    return lax.dot_general(a, b, NT, preferred_element_type=F32)


def kernel(
    tok, wq, wk, wv, om, wo, out,
    tokv, wqv, wkv, omv, wof, kf, qf, vv, omw, run, sloc, acc, res,
    r0, ma, ra, ma2, ra2, mb, rb, mb2, rb2, pa, ua, pb, ps, pf, pw, atts, attb,
    lsem, s0, q0, s1a, q1a, s1b, q1b, s2a, q2a, s2b, q2b, s3, q3, sA, qA,
    wss, wqs, wsp, wqp,
):
    seq, x = lax.axis_index("seq"), lax.axis_index("head")
    z, y, c = lax.div(seq, 8), lax.rem(lax.div(seq, 2), 4), lax.rem(seq, 2)

    def ahead(v, o):
        return lax.rem(v + o, 4)

    def dev(z_, y_, c_, x_):
        return {"seq": z_ * 8 + y_ * 2 + c_, "head": x_}

    partner = dev(z, y, 1 - c, x)
    ydev = [dev(z, ahead(y, o), c, x) for o in (1, 2, 3)]
    zdev = [dev(ahead(z, o), y, c, x) for o in (1, 2, 3)]
    xdev = [dev(z, y, c, ahead(x, o)) for o in (1, 2, 3)]

    def remote(src, dst, ss, rs, to):
        return pltpu.make_async_remote_copy(
            src_ref=src, dst_ref=dst, send_sem=ss, recv_sem=rs, device_id=to, device_id_type=MESH
        )

    def load(src, dst, i):
        copy = pltpu.make_async_copy(src, dst, lsem.at[i])
        copy.start()
        return copy

    def rows_of(j):
        return pl.ds(j * CHUNK, CHUNK)

    load_om = load(om, omv, 0)
    load_tok, load_kv = [], []
    def load_group(g):
        cols = pl.ds(g * NH * 128, NH * 128)
        load_kv.append(
            (
                load(wk.at[:, cols], wkv.at[g, :, pl.ds(0, NH * 128)], 5 + 2 * g),
                load(wv.at[:, cols], wkv.at[g, :, pl.ds(NH * 128, NH * 128)], 6 + 2 * g),
            )
        )

    load_tok.append(load(tok.at[rows_of(0)], tokv.at[rows_of(0)], 1))
    load_group(0)
    for j in range(1, 4):
        load_tok.append(load(tok.at[rows_of(j)], tokv.at[rows_of(j)], 1 + j))
    load_q = []

    barrier = pltpu.get_barrier_semaphore()
    for to in [partner] + ydev + zdev + xdev:
        pl.semaphore_signal(barrier, inc=1, device_id=to, device_id_type=MESH)

    for copy in [load_tok[0], *load_kv[0]]:
        copy.wait()
    held = [dot(tokv[rows_of(0)], wkv[0])]
    load_om.wait()

    scale = 128.0**-0.25
    omega = omv[...] * (scale * LOG2E)
    om_hi = omega.astype(BF)
    om_lo = (omega - om_hi.astype(F32)).astype(BF)
    omw[pl.ds(0, 128)] = om_hi
    omw[pl.ds(128, 128)] = om_hi
    omw[pl.ds(256, 128)] = om_lo
    omw[pl.ds(384, 128)] = jnp.full((128, 256), -1.0, BF)

    low = lax.broadcasted_iota(jnp.int32, (CHUNK, 128), 1) < 64

    def features(p):
        hi = p.astype(BF)
        lo = (p - hi.astype(F32)).astype(BF)
        square = p * p * (0.5 * scale * scale * LOG2E)
        pair = square + pltpu.roll(square, 64, 1) + 4.0 / 64
        pair_hi = pair.astype(BF).astype(F32)
        sums = jnp.where(low, pair_hi, pair - pair_hi).astype(BF)
        power = dot(jnp.concatenate([hi, lo, hi, sums], axis=1), omw[...])
        return (jnp.exp2(power) + 0.001 / 16).astype(BF)

    pl.semaphore_wait(barrier, 10)

    half = c * 256
    mine = lax.select(c == 0, y, z)

    def piece(o, start=0, size=PIECE):
        return pl.ds(pl.multiple_of(half + DIRECT + ahead(mine, o) * PIECE + start, 16), size)

    def along(o):
        return dev(
            lax.select(c == 0, z, ahead(z, o)), lax.select(c == 0, ahead(y, o), y), c, x
        )

    ends, sides = [along(1), along(3)], [xdev[0], xdev[2]]
    shard = [wof.at[ahead(x, o)] for o in (3, 1, 2)]
    direct = pl.ds(pl.multiple_of(half, 64), DIRECT)
    direct_parts = [pl.ds(pl.multiple_of(half + d * 32, 32), 32) for d in range(2)]
    piece_parts = [(0, HALF[0]), (HALF[0], HALF[1])]

    def passes(k, i, d, span, to, from_wo=False):
        where = wof.at[x, span] if from_wo else shard[i].at[span]
        return remote(wo.at[span] if from_wo else where, where, wss.at[k, i, d], wqs.at[k, i, d], to)

    w_x1 = [passes(0, 0, d, piece(0), sides[d], True) for d in range(2)]
    w_d1 = [passes(0, 1, d, direct, sides[d], True) for d in range(2)]
    w_x2 = [passes(1, d, 0, piece(0, *piece_parts[d]), sides[d]) for d in range(2)]
    w_d2 = [passes(1, d, 1, direct_parts[d], sides[d]) for d in range(2)]
    w_y = [[passes(2, i, d, piece(0), ends[d]) for d in range(2)] for i in range(3)]
    w_z = [[passes(3, i, d, piece(3 - 2 * d, *piece_parts[d]), ends[d]) for d in range(2)] for i in range(3)]
    w_p = [
        [
            remote(shard[i].at[span], shard[i].at[span], wsp.at[i, n], wqp.at[i, n], partner)
            for n, span in enumerate(
                [piece(0), piece(3), piece(1), piece(2, *piece_parts[0]), piece(2, *piece_parts[1]), direct]
            )
        ]
        for i in range(3)
    ]
    for copy in w_x1 + w_d1:
        copy.start()
    for g in range(1, GROUPS):
        load_group(g)

    def w_along_head(i):
        w_x1[i].wait_recv()
        w_x2[i].start()

    def w_along_head_direct(i):
        w_d1[i].wait_recv()
        w_d2[i].start()

    def w_first(i):
        if i == 2:
            for copy in w_x2:
                copy.wait_recv()
        w_y[i][0].start()
        w_y[i][1].start()

    def w_second(i):
        for d in range(2):
            w_y[i][d].wait_recv()
            w_z[i][d].start()
            w_p[i][1 + d].start()

    def w_third(i):
        for d in range(2):
            w_z[i][d].wait_recv()
            w_p[i][3 + d].start()

    def key_value(g, j, both):
        rows = rows_of(j)
        for i in range(NH):
            h = g * NH + i
            feat = features(both[:, i * 128 : (i + 1) * 128])
            v = both[:, (NH + i) * 128 : (NH + i + 1) * 128]
            kf[rows, h * 256 : (h + 1) * 256] = feat
            vv[rows, h * 128 : (h + 1) * 128] = v.astype(BF)
            turned = v.T.astype(BF)
            norm = jnp.ones((16, CHUNK), BF)
            state = dot(jnp.concatenate([turned[:64], norm, turned[64:], norm], axis=0), feat)
            for a in range(2):
                for l in range(2):
                    part = state[a * 80 : a * 80 + 80, l * 128 : (l + 1) * 128]
                    if j > 0:
                        so_far = run[l, h, a]
                        sloc[j, h, a * 80 : a * 80 + 80, l * 128 : (l + 1) * 128] = so_far.astype(BF)
                        part = so_far + part
                    run[l, h, a] = part

    causal = lax.broadcasted_iota(jnp.int32, (CHUNK, CHUNK), 0) >= lax.broadcasted_iota(
        jnp.int32, (CHUNK, CHUNK), 1
    )
    ones = jnp.ones((CHUNK, 128), BF)

    def query(n, j, q):
        rows = rows_of(j)
        for i in range(2):
            h = n * 2 + i
            qf[rows, h * 256 : (h + 1) * 256] = features(q[:, i * 128 : (i + 1) * 128])

    def inside(g, j):
        rows = rows_of(j)
        for h in range(g * NH, (g + 1) * NH):
            feat = qf[rows, h * 256 : (h + 1) * 256]
            scores = dot_nt(feat, kf[rows, h * 256 : (h + 1) * 256])
            weights = jnp.where(causal, scores, 0.0).astype(BF)
            value = jnp.concatenate([vv[rows, h * 128 : (h + 1) * 128], ones], axis=1)
            total = dot(weights, value)
            if j > 0:
                local = sloc[j, h]
                norm = local[64:80]
                total = total + dot_nt(
                    feat, jnp.concatenate([local[:64], local[80:144]] + [norm] * 8, axis=0)
                )
            acc[h, rows] = total

    def heads(g):
        return pl.ds(g * NH, NH)

    def round0(g):
        return remote(run.at[1 - c, heads(g)], r0.at[heads(g)], s0.at[g], q0.at[g], partner)

    def round1(g):
        return (
            [remote(ma.at[heads(g)], ra.at[i, heads(g)], s1a.at[g, i], q1a.at[g, i], ydev[i]) for i in range(3)],
            [remote(mb.at[heads(g)], rb.at[i, heads(g)], s1b.at[g, i], q1b.at[g, i], zdev[i]) for i in range(3)],
        )

    def round2(g):
        return (
            [remote(ma2.at[heads(g)], ra2.at[i, heads(g)], s2a.at[g, i], q2a.at[g, i], zdev[i]) for i in range(3)],
            [
                remote(
                    mb2.at[lax.select(y + i + 1 < 4, 1, 0), heads(g)], rb2.at[i, heads(g)],
                    s2b.at[g, i], q2b.at[g, i], ydev[i],
                )
                for i in range(3)
            ],
        )

    def round3(g):
        return remote(ps.at[heads(g)], pf.at[c, heads(g)], s3.at[g], q3.at[g], partner)

    def start1(g):
        hs = heads(g)
        round0(g).wait()
        chip = run[c, hs] + r0[hs]
        ua[hs] = chip[:, 0]
        ma[hs] = chip[:, 0].astype(BF)
        mb[hs] = chip[:, 1].astype(BF)
        over_y, over_z = round1(g)
        for i in range(3):
            over_y[i].start()
            pl.when(z + i + 1 < 4)(over_z[i].start)

    def start2(g):
        hs = heads(g)
        over_y, over_z = round1(g)
        pa[hs] = jnp.zeros((NH, 80, 128), F32)
        pb[hs] = jnp.zeros((NH, 80, 128), F32)
        for i in range(3):
            over_y[i].wait()
            got = ra[i, hs].astype(F32)
            ua[hs] += got
            pa[hs] += jnp.where(y >= i + 1, got, 0.0)
            pl.when(z + i + 1 < 4)(over_z[i].wait_send)

            @pl.when(z >= i + 1)
            def _():
                over_z[i].wait_recv()
                pb[hs] += rb[i, hs].astype(F32)

        ma2[hs] = ua[hs].astype(BF)
        mb2[0, hs] = pb[hs].astype(BF)
        mb2[1, hs] = (pb[hs] + mb[hs].astype(F32)).astype(BF)
        over_z, over_y = round2(g)
        for i in range(3):
            over_y[i].start()
            pl.when(z + i + 1 < 4)(over_z[i].start)

    def start3(g):
        hs = heads(g)
        over_z, over_y = round2(g)
        for i in range(3):
            over_y[i].wait()
            pb[hs] += rb2[i, hs].astype(F32)
            pl.when(z + i + 1 < 4)(over_z[i].wait_send)

            @pl.when(z >= i + 1)
            def _():
                over_z[i].wait_recv()
                pa[hs] += ra2[i, hs].astype(F32)

        for a, part in enumerate((pa, pb)):
            before = part[hs]
            ps[hs, a] = jnp.where(c == 0, before + run[c, hs, a], before).astype(BF)
            pf[c, hs, a] = jnp.where(c == 1, before + r0[hs, a], before).astype(BF)
        round3(g).start()

    def exchange(g, o):
        return remote(atts.at[o, :, pl.ds(g * NH * 128, NH * 128)], attb.at[o - 1, :, pl.ds(g * NH * 128, NH * 128)], sA.at[g, o - 1], qA.at[g, o - 1], xdev[o - 1])

    def combine(g):
        round3(g).wait()
        for h in range(g * NH, (g + 1) * NH):
            for l in range(2):
                norm = pf[l, h, 0, 64:80]
                pw[h, :, l * 128 : (l + 1) * 128] = jnp.concatenate(
                    [pf[l, h, 0, 0:64], pf[l, h, 1, 0:64]] + [norm] * 8, axis=0
                )
        order = (2, 1, 3, 0)
        totals = []
        for o in order:
            rows = pl.ds(pl.multiple_of(ahead(x, o) * CHUNK, CHUNK), CHUNK)
            for h in range(g * NH, (g + 1) * NH):
                totals.append(acc[h, rows] + dot_nt(qf[rows, h * 256 : (h + 1) * 256], pw[h]))
        for o in order:
            for h in range(g * NH, (g + 1) * NH):
                total = totals.pop(0)
                atts[o, :, h * 128 : (h + 1) * 128] = (total[:, :128] / total[:, 128:]).astype(BF)
        for o in order[:3]:
            exchange(g, o).start()

    def project(o, start, stop):
        source = ahead(x, 4 - o) if o else x
        att = attb[o - 1, :, start:stop] if o else atts[0, :, start:stop]
        return dot(att, wof[source, start:stop])

    stages = [("kv", g, j) for g in range(GROUPS) for j in range(4)]
    stages += [("q", n, j) for n in range(2) for j in range(4)]

    def front(kind, g, j):
        return dot(tokv[rows_of(j)], wqv[g] if kind == "q" else wkv[g])

    def step(count=1):
        for _ in range(count):
            (kind, g, j), wide = stages.pop(0), held.pop(0)
            if stages:
                held.append(front(*stages[0]))
            (query if kind == "q" else key_value)(g, j, wide)

    def insides(g):
        for j in range(4):
            inside(g, j)

    for copy in load_tok[1:3]:
        copy.wait()
    step(2)
    for copy in [load_tok[3], *load_kv[1]]:
        copy.wait()
    step(2)
    round0(0).start()
    for n in range(2):
        load_q.append(load(wq.at[:, pl.ds(n * 256, 256)], wqv.at[n], 13 + n))
    load_o = load(wo, wof.at[x], 15)
    for g in range(2, GROUPS):
        for copy in load_kv[g]:
            copy.wait()
    step(2)
    start1(0)
    step(2)
    round0(1).start()
    step(2)
    start1(1)
    step(2)
    round0(2).start()
    w_along_head(0)
    w_along_head(1)
    step(2)
    start2(0)
    start1(2)
    load_q[0].wait()
    load_q[1].wait()
    step(2)
    round0(3).start()
    step(2)
    start2(1)
    start1(3)
    step(2)
    w_first(0)
    start3(0)
    w_along_head_direct(0)
    w_along_head_direct(1)
    insides(0)
    start2(2)
    combine(0)
    w_first(1)
    insides(1)
    start3(1)
    start2(3)
    step(2)
    w_first(2)
    combine(1)
    for i in range(2):
        w_p[i][0].start()
        w_p[i][5].start()
    step(2)
    w_second(0)
    insides(2)
    start3(2)
    insides(3)
    combine(2)
    w_second(1)
    start3(3)
    load_o.wait()
    res[...] = project(0, 0, 256)
    w_p[2][0].start()
    combine(3)
    w_second(2)
    for copy in w_d2:
        copy.wait_recv()
    w_p[2][5].start()
    w_third(0)
    res[...] += project(0, 256, 512)
    w_third(1)
    for i in range(3):
        o = (1, 3, 2)[i]
        if i == 1:
            w_third(2)
        for copy in w_p[i]:
            copy.wait_recv()
        for g in range(2):
            exchange(g, o).wait()
        if i < 2:
            res[...] += project(o, 0, 256)
        if i == 1:
            for near in (1, 3):
                for g in range(2, 4):
                    exchange(g, near).wait()
                res[...] += project(near, 256, 512)
    for g in range(2, 4):
        exchange(g, 2).wait()
    out[...] = (res[...] + project(2, 0, 512)).astype(BF)
    for copy in w_x1 + w_d1 + w_x2 + w_d2 + sum(w_y + w_z + w_p, []):
        copy.wait_send()


def shards(tokens, w_query, w_key, w_value, omega, w_out):
    dma = pltpu.SemaphoreType.DMA
    V = pltpu.VMEM
    part = (4, 80, 128)
    whole = (4, 2, 80, 128)
    return pl.pallas_call(
        kernel,
        out_shape=jax.ShapeDtypeStruct((CHUNK, 2048), BF),
        in_specs=[pl.BlockSpec(memory_space=pltpu.HBM)] * 6,
        out_specs=pl.BlockSpec(memory_space=pltpu.VMEM),
        scratch_shapes=[
            V((1024, 2048), BF), V((2, 2048, 256), BF), V((GROUPS, 2048, NH * 256), BF), V((128, 256), F32),
            V((4, 512, 2048), BF), V((1024, 1024), BF), V((1024, 1024), BF), V((1024, 512), BF),
            V((512, 256), BF), V((2,) + whole, F32), V((4, 4, 160, 256), BF),
            V((4, 1024, 256), F32), V((CHUNK, 2048), F32),
            V(whole, F32), V(part, BF), V((3,) + part, BF), V(part, BF), V((3,) + part, BF),
            V(part, BF), V((3,) + part, BF), V((2,) + part, BF), V((3,) + part, BF),
            V(part, F32), V(part, F32), V(part, F32),
            V(whole, BF), V((2,) + whole, BF), V((4, 256, 256), BF),
            V((4, CHUNK, 512), BF), V((3, CHUNK, 512), BF),
            dma((16,)), dma((GROUPS,)), dma((GROUPS,)),
            dma((GROUPS, 3)), dma((GROUPS, 3)), dma((GROUPS, 3)), dma((GROUPS, 3)),
            dma((GROUPS, 3)), dma((GROUPS, 3)), dma((GROUPS, 3)), dma((GROUPS, 3)),
            dma((GROUPS,)), dma((GROUPS,)), dma((GROUPS, 3)), dma((GROUPS, 3)),
            dma((4, 3, 2)), dma((4, 3, 2)), dma((3, 6)), dma((3, 6)),
        ],
        compiler_params=pltpu.CompilerParams(
            collective_id=0, has_side_effects=True, vmem_limit_bytes=42 << 20
        ),
        name="causal_linear",
    )(*[pltpu.with_memory_space_constraint(a, pltpu.HBM) for a in (tokens, w_query, w_key, w_value, omega, w_out)])


def solution(mesh):
    placed = (
        P("seq", None), P(None, "head"), P(None, "head"), P(None, "head"), P(), P("head", None),
    )
    return jax.shard_map(
        shards, mesh=mesh, in_specs=placed, out_specs=P(("seq", "head"), None), check_vma=False
    )
```
